32 devices in a mesh: lon: 16 (over z, x, core), lat: 2 (over y).
Axes of the slice: x: 2, y: 2, z: 4, core: 2. Of those that a mesh axis runs over, the one named last changes fastest.
Arguments:
- fields: bfloat16 [64, 1792, 256], P('lat', 'lon'), may hold values from -6 to 6
- cotangent: bfloat16 [64, 1792, 256], P('lat', 'lon'), may hold values from -6 to 6
- kernel: float32 [31, 256], replicated, may hold values from -1 to 1
- up_weight: bfloat16 [256, 1024], replicated, may hold values from -0.375 to 0.375
- down_weight: bfloat16 [1024, 256], replicated, may hold values from -0.1875 to 0.1875
Outputs:
- output: bfloat16 [64, 1792, 256], P('lat', 'lon')
- field_grad: bfloat16 [64, 1792, 256], P('lat', 'lon')
- kernel_grad: float32 [31, 256], replicated
- up_grad: float32 [256, 1024], replicated
- down_grad: float32 [1024, 256], replicated
The draws below stay inside these ranges and needn't reach their ends.
All inputs are finite; a program needn't handle non-finite values.
Results may differ from the reference program's by a relative error of at most 0.0055.
Values may be sent and summed in bfloat16 or wider, within the bound.
No kernel may reach another device: no remote copies, remote signals or barrier semaphores. Data moves between devices by JAX's collectives and lax.ppermute only.
A program may use at most 128 MiB of HBM per device.

```python
import math
import jax
import jax.numpy as jnp
from jax import lax

C = 256
HID = 1024
KERNEL_TAPS = 31
KERNEL_SPACING = 4
W = 1792
LAT = 64


def levels(stream_key, dims, pieces, smallest, top_value):
    gain = 1.0
    for position, blocks in pieces:
        draws = jax.random.uniform(jax.random.fold_in(jax.random.fold_in(stream_key, 6), position), (blocks,), jnp.float32, smallest / len(pieces), top_value / len(pieces))
        gain = gain * jnp.repeat(jnp.exp(draws), dims[position] // blocks).reshape((-1,) + (1,) * (len(dims) - 1 - position))
    return gain


def centred(stream_key, dims, width, limit, split=(), held_as=jnp.bfloat16):
    result = width * jax.random.normal(stream_key, dims, jnp.float32)
    if split:
        result = result * levels(stream_key, dims, split, -0.22, 0.18)
    return jnp.clip(result, -limit, limit).astype(held_as)


def setup_inputs(seed: int = 0) -> dict:
    streams_of = jax.random.split(jax.random.key(seed), 6)
    fields = centred(streams_of[0], (LAT, W, C), 1.0, 6.0, ((0, 2), (1, 16)))
    cotangent = centred(streams_of[1], (LAT, W, C), 1.0, 6.0, ((0, 2), (1, 16)))
    kernel = centred(streams_of[2], (KERNEL_TAPS, C), KERNEL_TAPS ** -0.5, 1.0, (), jnp.float32)
    up_weight = centred(streams_of[3], (C, HID), C ** -0.5, 0.375)
    down_weight = centred(streams_of[4], (HID, C), HID ** -0.5, 0.1875)
    return dict(fields=fields, cotangent=cotangent, kernel=kernel, up_weight=up_weight, down_weight=down_weight)


def gelu_tanh(values):
    return jax.nn.gelu(values, approximate=True)

def reference(fields, cotangent, kernel, up_weight, down_weight):
    taps_half_span = KERNEL_TAPS // 2
    column_offsets = [KERNEL_SPACING * (index_of_tap - taps_half_span) for index_of_tap in range(KERNEL_TAPS)]

    def one_row(carry, inputs):
        row_in, row_cot = inputs
        row_float = row_in.astype(jnp.float32)
        conv = jnp.zeros(row_float.shape, jnp.float32)
        for index_of_tap in range(KERNEL_TAPS):
            conv = conv + kernel[index_of_tap] * jnp.roll(row_float, -column_offsets[index_of_tap], axis=0)
        center = lax.optimization_barrier(jnp.mean(conv, axis=-1, keepdims=True))
        deviation = conv - center
        spread = lax.optimization_barrier(jnp.mean(deviation * deviation, axis=-1, keepdims=True))
        inv_scale = lax.rsqrt(spread + 1e-06)
        normed = deviation * inv_scale
        normed_low = normed.astype(jnp.bfloat16)
        hidden = jnp.dot(normed_low, up_weight, preferred_element_type=jnp.float32)
        activated, pullback = jax.vjp(gelu_tanh, hidden)
        activated_low = activated.astype(jnp.bfloat16)
        output_row = (row_float + jnp.dot(activated_low, down_weight, preferred_element_type=jnp.float32)).astype(jnp.bfloat16)
        upstream = jnp.dot(row_cot, down_weight.T, preferred_element_type=jnp.float32)
        hidden_grad = pullback(upstream)[0].astype(jnp.bfloat16)
        grad_down = carry[2] + jnp.dot(activated_low.T, row_cot, preferred_element_type=jnp.float32)
        grad_up = carry[1] + jnp.dot(normed_low.T, hidden_grad, preferred_element_type=jnp.float32)
        normed_grad = jnp.dot(hidden_grad, up_weight.T, preferred_element_type=jnp.float32)
        mean_grad = lax.optimization_barrier(jnp.mean(normed_grad, axis=-1, keepdims=True))
        mean_cross = lax.optimization_barrier(jnp.mean(normed_grad * normed, axis=-1, keepdims=True))
        conv_grad = inv_scale * (normed_grad - mean_grad - normed * mean_cross)
        kernel_terms = jnp.stack([lax.optimization_barrier(jnp.sum(jnp.roll(row_float, -column_offsets[index_of_tap], axis=0) * conv_grad, axis=0)) for index_of_tap in range(KERNEL_TAPS)])
        back = row_cot.astype(jnp.float32)
        for index_of_tap in range(KERNEL_TAPS):
            back = back + kernel[index_of_tap] * jnp.roll(conv_grad, column_offsets[index_of_tap], axis=0)
        return ((carry[0] + kernel_terms, grad_up, grad_down), (output_row, back.astype(jnp.bfloat16)))
    start = (jnp.zeros((KERNEL_TAPS, C), jnp.float32), jnp.zeros((C, HID), jnp.float32), jnp.zeros((HID, C), jnp.float32))
    grads, rows_out = lax.scan(one_row, start, (fields, cotangent))
    factor = 1.0 / math.sqrt(LAT * W)
    return (rows_out[0], rows_out[1], grads[0] * factor, grads[1] * factor, grads[2] * factor)
```

```python
import functools
import math

import jax
import jax.numpy as jnp
from jax import lax
from jax.experimental import pallas as pl
from jax.experimental.pallas import tpu as pltpu
from jax.sharding import PartitionSpec as P

KERNEL_SPACING = 4
AXES = ("lon", "lat")
F32 = jnp.float32
BF16 = jnp.bfloat16
GELU_A = math.sqrt(2.0 / math.pi)
GELU_B = GELU_A * 0.044715


def xor_permute(value, mask):
    nlon, nlat = lax.axis_size("lon"), lax.axis_size("lat")
    lat_mask, lon_mask = mask
    pairs = [
        (lon * nlat + lat, (lon ^ lon_mask) * nlat + (lat ^ lat_mask))
        for lon in range(nlon)
        for lat in range(nlat)
    ]
    return lax.ppermute(value, AXES, pairs)


def passed_along(value, by):
    count = lax.axis_size("lon")
    return lax.ppermute(value, "lon", [(i, (i + by) % count) for i in range(count)])


def groups():
    nlon, nlat = lax.axis_size("lon"), lax.axis_size("lat")
    lon, lat = lax.axis_index("lon"), lax.axis_index("lat")
    core = (2, lon % 2, [(0, s) for s in range(2)])
    plane = (2 * nlat, lat * 2 + (lon // 2) % 2, [(s >> 1, (s & 1) * 2) for s in range(2 * nlat)])
    depth = (nlon // 4, lon // 4, [(0, s * 4) for s in range(nlon // 4)])
    return core, plane, depth


def scatter_stage(value, group):
    size, own, masks = group
    parts = value.reshape(size, value.shape[0] // size, value.shape[1])
    sends = [
        lax.dynamic_index_in_dim(parts, own ^ s, 0, keepdims=False).astype(BF16)
        for s in range(1, size)
    ]
    total = lax.dynamic_index_in_dim(parts, own, 0, keepdims=False)
    for s in range(1, size):
        total = total + xor_permute(sends[s - 1], masks[s]).astype(F32)
    return total


def gather_stage(value, extra, group):
    size, own, masks = group
    rows = value.shape[0]
    packed = jnp.concatenate([value, extra.astype(BF16)], axis=0)
    got = [value]
    for s in range(1, size):
        part = xor_permute(packed, masks[s])
        got.append(part[:rows])
        extra = extra + part[rows:].astype(F32)
    whole = jnp.zeros((size,) + value.shape, value.dtype)
    for s in range(size):
        whole = lax.dynamic_update_index_in_dim(whole, got[s], own ^ s, 0)
    return whole.reshape(size * rows, value.shape[1]), extra


def stage_row(s0, s4, left, middle, right):
    edge, cols = left.shape[0], middle.shape[0]
    left, middle, right = left.astype(F32), middle.astype(F32), right.astype(F32)
    s0[pl.ds(0, edge), :] = left
    s0[pl.ds(edge, cols), :] = middle
    s0[pl.ds(edge + cols, edge), :] = right
    s4[pl.ds(0, edge - 4), :] = left[4:]
    s4[pl.ds(edge - 4, cols), :] = middle
    s4[pl.ds(edge - 4 + cols, edge), :] = right


def spread_taps(kb, kernel_ref, taps, flip):
    for t in range(taps):
        row = kernel_ref[pl.ds(taps - 1 - t if flip else t, 1), :]
        kb[t] = jnp.broadcast_to(row, kb.shape[1:])


def conv_lane(s0, s4, kb, lane, cols, taps):
    blocks = cols // 8
    lanes = pl.ds(lane * 128, 128)
    acc = [None] * blocks
    weights = [kb[t, :, lanes] for t in range(taps)]
    for i in range(blocks + taps // 2):
        for half, ref in ((0, s0), (1, s4)):
            uses = [(j, 2 * (i - j) + half) for j in range(blocks) if 0 <= 2 * (i - j) + half < taps]
            if not uses:
                continue
            x = ref[pl.ds(8 * i, 8), lanes]
            for j, t in uses:
                term = weights[t] * x
                acc[j] = term if acc[j] is None else acc[j] + term
    return acc


def forward_kernel(
    fields_ref, left_ref, right_ref, cot_ref, kernel_ref, up_ref, upt_ref, down_ref, downt_ref,
    out_ref, grad_ref, edge_left_ref, edge_right_ref, gup_ref, gdown_ref,
    s0, s4, kb, conv_s, normed_s, gdt_s,
):
    step = pl.program_id(0)
    rows, cols, channels = fields_ref.shape
    edge = left_ref.shape[1]
    taps = kernel_ref.shape[0]
    hidden_size = up_ref.shape[1]
    cells = rows * cols
    width = 256

    @pl.when(step == 0)
    def _():
        spread_taps(kb, kernel_ref, taps, False)
        gup_ref[...] = jnp.zeros_like(gup_ref)
        gdt_s[...] = jnp.zeros_like(gdt_s)

    def one_row(r, carry):
        stage_row(s0, s4, left_ref[r], fields_ref[r], right_ref[r])
        for lane in range(channels // 128):
            acc = conv_lane(s0, s4, kb, lane, cols, taps)
            for j, value in enumerate(acc):
                conv_s[r, pl.ds(8 * j, 8), pl.ds(lane * 128, 128)] = value
        return carry

    lax.fori_loop(0, rows, one_row, 0)

    conv = conv_s[...].reshape(cells, channels)
    center = jnp.mean(conv, axis=-1, keepdims=True)
    deviation = conv - center
    spread = jnp.mean(deviation * deviation, axis=-1, keepdims=True)
    inv_scale = lax.rsqrt(spread + 1e-06)
    normed = deviation * inv_scale
    normed_s[...] = normed
    low = normed.astype(BF16)
    cot = cot_ref[...].reshape(cells, channels)
    first = (((0,), (0,)), ((), ()))
    out = fields_ref[...].reshape(cells, channels).astype(F32)
    normed_grad = None
    for j in range(hidden_size // width):
        part = pl.ds(j * width, width)
        h = jnp.dot(low, up_ref[:, part], preferred_element_type=F32)
        u = jnp.dot(cot, downt_ref[:, part], preferred_element_type=F32)
        sq = h * h
        t = jnp.tanh(h * (GELU_A + GELU_B * sq))
        half = 0.5 * h
        act = (half + half * t).astype(BF16)
        slope = (0.5 + 0.5 * t) + half * (1.0 - t * t) * (GELU_A + (3.0 * GELU_B) * sq)
        hg = (u * slope).astype(BF16)
        out = out + jnp.dot(act, down_ref[part, :], preferred_element_type=F32)
        term = jnp.dot(hg, upt_ref[part, :], preferred_element_type=F32)
        normed_grad = term if normed_grad is None else normed_grad + term
        gup_ref[j] += lax.dot_general(low, hg, first, preferred_element_type=F32)
        gdt_s[:, part] += lax.dot_general(cot, act, first, preferred_element_type=F32)
    out_ref[...] = out.astype(BF16).reshape(rows, cols, channels)
    normed = normed_s[...]
    mean_grad = jnp.mean(normed_grad, axis=-1, keepdims=True)
    mean_cross = jnp.mean(normed_grad * normed, axis=-1, keepdims=True)
    grad = inv_scale * (normed_grad - mean_grad - normed * mean_cross)
    grad_ref[...] = grad.reshape(rows, cols, channels)
    edge_left_ref[...] = grad_ref[:, pl.ds(0, edge), :].astype(BF16)
    edge_right_ref[...] = grad_ref[:, pl.ds(cols - edge, edge), :].astype(BF16)

    @pl.when(step == pl.num_programs(0) - 1)
    def _():
        for j in range(hidden_size // width):
            part = pl.ds(j * width, width)
            gdown_ref[part, :] = gdt_s[:, part].T


def forward(fields, left, right, cot, kernel, up, down, block):
    rows, cols, channels = fields.shape
    edge, taps, hid = left.shape[1], kernel.shape[0], up.shape[1]
    by_row = lambda n: pl.BlockSpec((block, n, channels), lambda i: (i, 0, 0))
    whole = lambda *shape: pl.BlockSpec(shape, lambda i: (0,) * len(shape))
    padded = cols + 2 * edge
    cells = rows * cols
    return pl.pallas_call(
        forward_kernel,
        grid=(rows // block,),
        in_specs=[
            by_row(cols), by_row(edge), by_row(edge), by_row(cols), whole(taps, channels),
            whole(channels, hid), whole(hid, channels), whole(hid, channels), whole(channels, hid),
        ],
        out_specs=[
            by_row(cols), by_row(cols), by_row(edge), by_row(edge),
            whole(hid // 256, channels, 256), whole(hid, channels),
        ],
        out_shape=[
            jax.ShapeDtypeStruct((rows, cols, channels), BF16),
            jax.ShapeDtypeStruct((rows, cols, channels), F32),
            jax.ShapeDtypeStruct((rows, edge, channels), BF16),
            jax.ShapeDtypeStruct((rows, edge, channels), BF16),
            jax.ShapeDtypeStruct((hid // 256, channels, 256), F32),
            jax.ShapeDtypeStruct((hid, channels), F32),
        ],
        scratch_shapes=[
            pltpu.VMEM((padded, channels), F32),
            pltpu.VMEM((padded, channels), F32),
            pltpu.VMEM((taps, 8, channels), F32),
            pltpu.VMEM((block, cols, channels), F32),
            pltpu.VMEM((block * cols, channels), F32),
            pltpu.VMEM((channels, hid), F32),
        ],
        compiler_params=pltpu.CompilerParams(
            dimension_semantics=("arbitrary",), vmem_limit_bytes=50 * 2**20
        ),
        cost_estimate=pl.CostEstimate(
            flops=12 * cells * channels * hid, transcendentals=cells * hid,
            bytes_accessed=cells * channels * 12,
        ),
        name="forward",
    )(fields, left, right, cot, kernel, up, up.T, down, down.T)


def kernel_grad_kernel(fields_ref, left_ref, right_ref, grad_ref, out_ref, s0, s4, sums):
    step = pl.program_id(0)
    rows, cols, channels = fields_ref.shape
    taps = out_ref.shape[0] - 1
    blocks = cols // 8

    @pl.when(step == 0)
    def _():
        sums[...] = jnp.zeros_like(sums)

    def one_row(r, carry):
        stage_row(s0, s4, left_ref[r], fields_ref[r], right_ref[r])
        for lane in range(channels // 128):
            lanes = pl.ds(lane * 128, 128)
            grads = [grad_ref[r, pl.ds(8 * j, 8), lanes] for j in range(blocks)]
            acc = [None] * taps
            for i in range(blocks + taps // 2):
                for half, ref in ((0, s0), (1, s4)):
                    uses = [
                        (j, 2 * (i - j) + half)
                        for j in range(blocks)
                        if 0 <= 2 * (i - j) + half < taps
                    ]
                    if not uses:
                        continue
                    x = ref[pl.ds(8 * i, 8), lanes]
                    for j, t in uses:
                        term = grads[j] * x
                        acc[t] = term if acc[t] is None else acc[t] + term
            for t in range(taps):
                sums[t, :, lanes] += acc[t]
        return carry

    lax.fori_loop(0, rows, one_row, 0)

    @pl.when(step == pl.num_programs(0) - 1)
    def _():
        for t in range(taps):
            out_ref[pl.ds(t, 1), :] = jnp.sum(sums[t], axis=0, keepdims=True)
        out_ref[pl.ds(taps, 1), :] = jnp.zeros((1, channels), F32)


def kernel_grad(fields, left, right, grad, taps, block):
    rows, cols, channels = fields.shape
    edge = left.shape[1]
    by_row = lambda n: pl.BlockSpec((block, n, channels), lambda i: (i, 0, 0))
    return pl.pallas_call(
        kernel_grad_kernel,
        grid=(rows // block,),
        in_specs=[by_row(cols), by_row(edge), by_row(edge), by_row(cols)],
        out_specs=pl.BlockSpec((taps + 1, channels), lambda i: (0, 0)),
        out_shape=jax.ShapeDtypeStruct((taps + 1, channels), F32),
        scratch_shapes=[
            pltpu.VMEM((cols + 2 * edge, channels), F32),
            pltpu.VMEM((cols + 2 * edge, channels), F32),
            pltpu.VMEM((taps, 8, channels), F32),
        ],
        compiler_params=pltpu.CompilerParams(
            dimension_semantics=("arbitrary",), vmem_limit_bytes=32 * 2**20
        ),
        cost_estimate=pl.CostEstimate(
            flops=2 * taps * rows * cols * channels, transcendentals=0,
            bytes_accessed=rows * cols * channels * 8,
        ),
        name="kernel_grad",
    )(fields, left, right, grad)


def backward_kernel(grad_ref, left_ref, right_ref, cot_ref, kernel_ref, out_ref, s0, s4, kb):
    rows, cols, channels = grad_ref.shape
    taps = kernel_ref.shape[0]

    @pl.when(pl.program_id(0) == 0)
    def _():
        spread_taps(kb, kernel_ref, taps, True)

    def one_row(r, carry):
        stage_row(s0, s4, left_ref[r], grad_ref[r], right_ref[r])
        for lane in range(channels // 128):
            acc = conv_lane(s0, s4, kb, lane, cols, taps)
            lanes = pl.ds(lane * 128, 128)
            back = jnp.concatenate(acc, axis=0) + cot_ref[r, :, lanes].astype(F32)
            out_ref[r, :, lanes] = back.astype(BF16)
        return carry

    lax.fori_loop(0, rows, one_row, 0)


def backward(grad, left, right, cot, kernel, block):
    rows, cols, channels = grad.shape
    edge, taps = left.shape[1], kernel.shape[0]
    by_row = lambda n: pl.BlockSpec((block, n, channels), lambda i: (i, 0, 0))
    return pl.pallas_call(
        backward_kernel,
        grid=(rows // block,),
        in_specs=[
            by_row(cols), by_row(edge), by_row(edge), by_row(cols),
            pl.BlockSpec((taps, channels), lambda i: (0, 0)),
        ],
        out_specs=by_row(cols),
        out_shape=jax.ShapeDtypeStruct((rows, cols, channels), BF16),
        scratch_shapes=[
            pltpu.VMEM((cols + 2 * edge, channels), F32),
            pltpu.VMEM((cols + 2 * edge, channels), F32),
            pltpu.VMEM((taps, 8, channels), F32),
        ],
        compiler_params=pltpu.CompilerParams(
            dimension_semantics=("arbitrary",), vmem_limit_bytes=32 * 2**20
        ),
        cost_estimate=pl.CostEstimate(
            flops=2 * taps * rows * cols * channels, transcendentals=0,
            bytes_accessed=rows * cols * channels * 10,
        ),
        name="backward",
    )(grad, left, right, cot, kernel)


def per_device(fields, cotangent, kernel, up_weight, down_weight):
    rows, cols, channels = fields.shape
    taps, hid = kernel.shape[0], up_weight.shape[1]
    edge = KERNEL_SPACING * (taps // 2)
    left = passed_along(fields[:, cols - edge :], 1)
    right = passed_along(fields[:, :edge], -1)
    output, grad, edge_left, edge_right, gup, gdown = forward(
        fields, left, right, cotangent, kernel, up_weight, down_weight, 4
    )
    core, plane, depth = groups()
    weights = jnp.concatenate([gup.reshape(hid, channels), gdown], axis=0)
    part = scatter_stage(weights, core)
    grad_left = passed_along(edge_right, 1)
    grad_right = passed_along(edge_left, -1)
    part = scatter_stage(part, plane)
    kgrad = kernel_grad(fields, left, right, grad, taps, 8)
    part = scatter_stage(part, depth).astype(BF16)
    field_grad = backward(grad, grad_left, grad_right, cotangent, kernel, 8)
    part, kgrad = gather_stage(part, kgrad, depth)
    part, kgrad = gather_stage(part, kgrad, plane)
    part, kgrad = gather_stage(part, kgrad, core)
    factor = 1.0 / math.sqrt(rows * cols * lax.axis_size("lon") * lax.axis_size("lat"))
    scaled = part.astype(F32) * factor
    up_grad = scaled[:hid].reshape(hid // 256, channels, 256).transpose(1, 0, 2).reshape(channels, hid)
    return (output, field_grad, kgrad[:taps] * factor, up_grad, scaled[hid:])


def solution(mesh):
    placed = (P("lat", "lon", None), P("lat", "lon", None), P(), P(), P())
    return jax.shard_map(
        per_device,
        mesh=mesh,
        in_specs=placed,
        out_specs=(P("lat", "lon", None), P("lat", "lon", None), P(), P(), P()),
        check_vma=False,
    )
```

```python
import functools
import math

import jax
import jax.numpy as jnp
from jax import lax
from jax.experimental import pallas as pl
from jax.experimental.pallas import tpu as pltpu
from jax.sharding import PartitionSpec as P

KERNEL_SPACING = 4
BLOCK = 4
AXES = ("lon", "lat")
F32 = jnp.float32
BF16 = jnp.bfloat16
GELU_A = math.sqrt(2.0 / math.pi)
GELU_B = GELU_A * 0.044715


def xor_permute(value, mask):
    nlon, nlat = lax.axis_size("lon"), lax.axis_size("lat")
    lat_mask, lon_mask = mask
    pairs = [
        (lon * nlat + lat, (lon ^ lon_mask) * nlat + (lat ^ lat_mask))
        for lon in range(nlon)
        for lat in range(nlat)
    ]
    return lax.ppermute(value, AXES, pairs)


def passed_along(value, by):
    count = lax.axis_size("lon")
    return lax.ppermute(value, "lon", [(i, (i + by) % count) for i in range(count)])


def groups():
    nlon, nlat = lax.axis_size("lon"), lax.axis_size("lat")
    lon, lat = lax.axis_index("lon").astype(jnp.uint32), lax.axis_index("lat").astype(jnp.uint32)
    core = (lon & 1, [(0, s) for s in range(2)])
    plane = (lat * 2 + ((lon >> 1) & 1), [(s >> 1, (s & 1) * 2) for s in range(2 * nlat)])
    depth = (lon >> 2, [(0, s * 4) for s in range(nlon // 4)])
    return [([own ^ jnp.uint32(s) for s in range(len(masks))], masks) for own, masks in (core, plane, depth)]


def piece(parts, place):
    zero = jnp.uint32(0)
    return lax.dynamic_slice(parts, (place, zero, zero), (1,) + parts.shape[1:])[0]


def scatter_stage(value, group):
    places, _ = group
    size = len(places)
    parts = value.reshape(size, value.shape[0] // size, value.shape[1])
    return [piece(parts, p).astype(BF16) for p in places[1:]], piece(parts, places[0])


def scatter_finish(sends, total, group):
    _, masks = group
    for send, mask in zip(sends, masks[1:]):
        total = total + xor_permute(send, mask).astype(F32)
    return total


def gather_finish(packed, extra, group):
    places, masks = group
    size = len(places)
    rows = packed.shape[0] - extra.shape[0]
    got = [packed[:rows]]
    for s in range(1, size):
        part = xor_permute(packed, masks[s])
        got.append(part[:rows])
        extra = extra + part[rows:].astype(F32)
    whole = jnp.zeros((size, rows, packed.shape[1]), packed.dtype)
    zero = jnp.uint32(0)
    for part, place in zip(got, places):
        whole = lax.dynamic_update_slice(whole, part[None], (place, zero, zero))
    return whole.reshape(size * rows, packed.shape[1]), extra


def pack(value, extra):
    return jnp.concatenate([value, extra.astype(BF16)], axis=0)


def lane_groups(channels):
    return range(channels // 128)


def stage_row(s0, s4, left, middle, right):
    edge, cols = left.shape[0], middle.shape[0]
    left, middle, right = left.astype(F32), middle.astype(F32), right.astype(F32)
    s0[pl.ds(0, edge), :] = left
    s0[pl.ds(edge, cols), :] = middle
    s0[pl.ds(edge + cols, edge), :] = right
    s4[pl.ds(0, edge - 4), :] = left[4:]
    s4[pl.ds(edge - 4, cols), :] = middle
    s4[pl.ds(edge - 4 + cols, edge - 4), :] = right[: edge - 4]


def spread_taps(kb, kernel_ref, flip):
    taps = kernel_ref.shape[0]
    for t in range(taps):
        row = kernel_ref[pl.ds(taps - 1 - t if flip else t, 1), :]
        kb[t] = jnp.broadcast_to(row, kb.shape[1:])


def tap_uses(blocks, taps, edge):
    lead = (edge - KERNEL_SPACING * (taps // 2)) // 4
    result = []
    for i in range(blocks + 2 * edge // 8):
        for half in (0, 1):
            uses = []
            for j in range(blocks):
                t = 2 * (i - j) + half - lead
                if 0 <= t < taps:
                    uses.append((j, t))
            if uses:
                result.append((i, half, uses))
    return result


def add_to(acc, at, term):
    acc[at] = term if acc[at] is None else acc[at] + term


def conv_lane(s0, s4, kb, lane, cols, taps, edge):
    lanes = pl.ds(lane * 128, 128)
    acc = [None] * (cols // 8)
    weights = [kb[t, :, lanes] for t in range(taps)]
    for i, half, uses in tap_uses(cols // 8, taps, edge):
        x = (s4 if half else s0)[pl.ds(8 * i, 8), lanes]
        for j, t in uses:
            add_to(acc, j, weights[t] * x)
    return acc


def row_spec(block, n, width):
    return pl.BlockSpec((block, n, width), lambda i: (i, 0, 0))


def whole_spec(*shape):
    return pl.BlockSpec(shape, lambda i: (0,) * len(shape))


def resident():
    return pl.BlockSpec(memory_space=pltpu.VMEM)


def resident_shape(*shape):
    return pltpu.VMEM(shape, F32)


def params(mib):
    return pltpu.CompilerParams(dimension_semantics=("arbitrary",), vmem_limit_bytes=mib * 2**20)


def inner_kernel(fields_ref, kernel_ref, up_hbm, down_hbm, out_ref, upt_ref, downt_ref, s0, s4, kb, up_ref, down_ref, sems):
    rows, cols, channels = fields_ref.shape
    taps = kernel_ref.shape[0]

    spread_taps(kb, kernel_ref, False)
    s4[...] = jnp.zeros_like(s4)
    copies = [
        pltpu.make_async_copy(up_hbm, up_ref, sems.at[0]),
        pltpu.make_async_copy(down_hbm, down_ref, sems.at[1]),
    ]
    for copy in copies:
        copy.start()

    def one_row(r, carry):
        middle = fields_ref[r].astype(F32)
        s0[...] = middle
        s4[pl.ds(4, cols), :] = middle
        for lane in lane_groups(channels):
            lanes = pl.ds(lane * 128, 128)
            weights = [kb[t, :, lanes] for t in range(taps)]
            acc = [None] * (cols // 8)
            for i in range(cols // 8 + 1):
                for half, ref in ((0, s0), (1, s4)):
                    if half == 0 and i == cols // 8:
                        continue
                    x = ref[pl.ds(8 * i, 8), lanes]
                    for j in range(cols // 8):
                        t = 2 * (i - j) - half + taps // 2
                        if 0 <= t < taps:
                            add_to(acc, j, weights[t] * x)
            for j, value in enumerate(acc):
                out_ref[r, pl.ds(8 * j, 8), lanes] = value
        return carry

    lax.fori_loop(0, rows, one_row, 0)

    for copy in copies:
        copy.wait()
    for j in range(up_ref.shape[1] // 256):
        part = pl.ds(256 * j, 256)
        upt_ref[part, :] = up_ref[:, part].T
        downt_ref[:, part] = down_ref[part, :].T


def inner(fields, kernel, up, down):
    rows, cols, channels = fields.shape
    taps = kernel.shape[0]
    return pl.pallas_call(
        inner_kernel,
        in_specs=[resident()] * 2 + [pl.BlockSpec(memory_space=pltpu.HBM)] * 2,
        out_specs=[resident()] * 3,
        out_shape=[resident_shape(rows, cols, channels), pltpu.VMEM(down.shape, BF16), pltpu.VMEM(up.shape, BF16)],
        scratch_shapes=[
            pltpu.VMEM((cols, channels), F32),
            pltpu.VMEM((cols + 8, channels), F32),
            pltpu.VMEM((taps, 8, channels), F32),
            pltpu.VMEM(up.shape, BF16),
            pltpu.VMEM(down.shape, BF16),
            pltpu.SemaphoreType.DMA((2,)),
        ],
        compiler_params=pltpu.CompilerParams(vmem_limit_bytes=8 * 2**20),
        cost_estimate=pl.CostEstimate(
            flops=260 * taps * rows * cols * channels, transcendentals=0,
            bytes_accessed=rows * cols * channels * 6,
        ),
        name="inner",
    )(fields, kernel, up, down)


def forward_kernel(
    first, last, start, core_ref, inner_ref, left_ref, right_ref, fields_ref, cot_ref, kernel_ref,
    up_ref, upt_ref, down_ref, downt_ref, *refs,
):
    given, refs = ((), refs) if first else (refs[:4], refs[4:])
    (out_ref, grad_ref, gup_ref, gdt_ref, edge_left_ref, edge_right_ref), refs = refs[:6], refs[6:]
    edges, kb, conv_s, normed_s, act_s, hg_s = refs[:6]
    gup_s, gdt_s = refs[6:] if last else (gup_ref, gdt_ref)
    step = pl.program_id(0)
    rows, edge, _ = left_ref.shape
    _, cols, channels = inner_ref.shape
    base_row = start + step * rows
    here = pl.ds(base_row, rows)
    taps = kernel_ref.shape[0]
    hid = up_ref.shape[1]
    cells = rows * cols
    blocks, reach = cols // 8, taps // 2
    width = 256

    @pl.when(step == 0)
    def _():
        spread_taps(kb, kernel_ref, False)
        gup_s[...] = jnp.zeros_like(gup_s) if first else given[2][...]
        gdt_s[...] = jnp.zeros_like(gdt_s) if first else given[3][...]
        edges[...] = jnp.zeros_like(edges)

    def one_row(r, carry):
        left, right = left_ref[r].astype(F32), right_ref[r].astype(F32)
        edges[0] = left
        edges[1, pl.ds(0, edge - 4), :] = left[4:]
        edges[2] = right
        edges[3, pl.ds(4, edge - 4), :] = right[: edge - 4]
        for lane in lane_groups(channels):
            lanes = pl.ds(lane * 128, 128)
            weights = [kb[t, :, lanes] for t in range(taps)]
            acc = [None] * blocks
            for which in range(4):
                for i in range(edge // 8):
                    column = (-edge, 4 - edge, cols, cols - 4)[which] + 8 * i
                    x = None
                    for j in range(blocks):
                        t = (column - 8 * j) // 4 + reach
                        if 0 <= t < taps:
                            if x is None:
                                x = edges[which, pl.ds(8 * i, 8), lanes]
                            add_to(acc, j, weights[t] * x)
            for j, value in enumerate(acc):
                base = inner_ref[base_row + r, pl.ds(8 * j, 8), lanes]
                conv_s[r, pl.ds(8 * j, 8), lanes] = base if value is None else base + value
        return carry

    lax.fori_loop(0, rows, one_row, 0)

    conv = conv_s[...].reshape(cells, channels)
    center = jnp.mean(conv, axis=-1, keepdims=True)
    deviation = conv - center
    spread = jnp.mean(deviation * deviation, axis=-1, keepdims=True)
    inv_scale = lax.rsqrt(spread + 1e-06)
    normed = deviation * inv_scale
    normed_s[...] = normed
    low = normed.astype(BF16)
    cot = cot_ref[...].reshape(cells, channels)
    over_cells = (((0,), (0,)), ((), ()))
    for j in range(hid // width):
        part = pl.ds(j * width, width)
        h = jnp.dot(low, up_ref[:, part], preferred_element_type=F32)
        u = jnp.dot(cot, downt_ref[:, part], preferred_element_type=F32)
        sq = h * h
        t = jnp.tanh(h * (GELU_A + GELU_B * sq))
        half = 0.5 * h
        act_s[:, part] = (half + half * t).astype(BF16)
        slope = (0.5 + 0.5 * t) + half * (1.0 - t * t) * (GELU_A + (3.0 * GELU_B) * sq)
        hg_s[:, part] = (u * slope).astype(BF16)
    out = jnp.dot(act_s[...], down_ref[...], preferred_element_type=F32)
    out = out + fields_ref[here].reshape(cells, channels).astype(F32)
    normed_grad = jnp.dot(hg_s[...], upt_ref[...], preferred_element_type=F32)
    for j in range(hid // width):
        part = pl.ds(j * width, width)
        gup_s[j] += lax.dot_general(low, hg_s[:, part], over_cells, preferred_element_type=F32)
        gdt_s[:, part] += lax.dot_general(cot, act_s[:, part], over_cells, preferred_element_type=F32)
    out_ref[...] = out.astype(BF16).reshape(rows, cols, channels)
    normed = normed_s[...]
    mean_grad = jnp.mean(normed_grad, axis=-1, keepdims=True)
    mean_cross = jnp.mean(normed_grad * normed, axis=-1, keepdims=True)
    grad = inv_scale * (normed_grad - mean_grad - normed * mean_cross)
    grad_ref[here] = grad.reshape(rows, cols, channels)
    edge_left_ref[...] = grad_ref[here, pl.ds(0, edge), :].astype(BF16)
    edge_right_ref[...] = grad_ref[here, pl.ds(cols - edge, edge), :].astype(BF16)

    if last:
        mine_ref, theirs_ref = gup_ref, gdt_ref
        ending = step == pl.num_programs(0) - 1

        @pl.when(ending & (core_ref[0] == 0))
        def _():
            for j in range(hid // width):
                part = pl.ds(j * width, width)
                mine_ref[part, :] = gup_s[j]
                theirs_ref[part, :] = gdt_s[:, part].T.astype(BF16)

        @pl.when(ending & (core_ref[0] == 1))
        def _():
            for j in range(hid // width):
                part = pl.ds(j * width, width)
                theirs_ref[part, :] = gup_s[j].astype(BF16)
                mine_ref[part, :] = gdt_s[:, part].T


def forward(core, conv_inner, left, right, fields, cot, kernel, up, up_t, down, down_t, carried, start, last):
    rows, cols, channels = cot.shape
    count, edge, _ = left.shape
    taps, hid = kernel.shape[0], up.shape[1]
    cells = count * cols
    block = BLOCK
    own = functools.partial(row_spec, block)
    at = lambda n: pl.BlockSpec((block, n, channels), lambda i: (i + start // block, 0, 0))
    anywhere = pl.BlockSpec(memory_space=pl.ANY)
    sums = [(hid // 256, channels, 256), (channels, hid)]
    ends = [((hid, channels), F32), ((hid, channels), BF16)] if last else [(s, F32) for s in sums]
    fixed = [
        pl.BlockSpec(memory_space=pltpu.SMEM),
        resident(), own(edge, channels), own(edge, channels), resident(), at(cols), resident(),
        resident(), resident(), resident(), resident(),
    ]
    return pl.pallas_call(
        functools.partial(forward_kernel, not carried, last, start),
        grid=(count // block,),
        in_specs=fixed + ([anywhere, resident(), resident(), resident()] if carried else []),
        out_specs=[at(cols)] + [resident()] * 3 + [own(edge, channels)] * 2,
        out_shape=[
            jax.ShapeDtypeStruct((rows, cols, channels), BF16),
            resident_shape(rows, cols, channels),
        ]
        + [pltpu.VMEM(s, d) for s, d in ends]
        + [jax.ShapeDtypeStruct((count, edge, channels), BF16)] * 2,
        input_output_aliases={11: 0, 12: 1} if carried else {},
        scratch_shapes=[
            pltpu.VMEM((4, edge, channels), F32),
            pltpu.VMEM((taps, 8, channels), F32),
            pltpu.VMEM((block, cols, channels), F32),
            pltpu.VMEM((block * cols, channels), F32),
            pltpu.VMEM((block * cols, hid), BF16),
            pltpu.VMEM((block * cols, hid), BF16),
        ]
        + ([pltpu.VMEM(s, F32) for s in sums] if last else []),
        compiler_params=params(20),
        cost_estimate=pl.CostEstimate(
            flops=28 * cells * channels * hid, transcendentals=cells * hid,
            bytes_accessed=cells * channels * 12,
        ),
        name="forward",
    )(core, conv_inner, left, right, fields, cot, kernel, up, up_t, down, down_t, *carried)


def kernel_grad_kernel(start, fields_ref, left_ref, right_ref, grad_ref, given_ref, out_ref, s0, s4, sums):
    _, cols, channels = fields_ref.shape
    rows, edge, _ = left_ref.shape
    taps = out_ref.shape[0] - 1
    blocks = cols // 8

    sums[...] = jnp.zeros_like(sums)

    def one_row(r, carry):
        stage_row(s0, s4, left_ref[r], fields_ref[start + r], right_ref[r])
        for lane in lane_groups(channels):
            lanes = pl.ds(lane * 128, 128)
            grads = [grad_ref[start + r, pl.ds(8 * j, 8), lanes] for j in range(blocks)]
            acc = [None] * taps
            for i, half, uses in tap_uses(blocks, taps, edge):
                x = (s4 if half else s0)[pl.ds(8 * i, 8), lanes]
                for j, t in uses:
                    add_to(acc, t, grads[j] * x)
            for t in range(taps):
                sums[t, :, lanes] += acc[t]
        return carry

    lax.fori_loop(0, rows, one_row, 0)

    for t in range(taps):
        here = jnp.sum(sums[t], axis=0, keepdims=True)
        out_ref[pl.ds(t, 1), :] = given_ref[pl.ds(t, 1), :] + here
    out_ref[pl.ds(taps, 1), :] = jnp.zeros((1, channels), F32)


def staging(cols, edge, channels):
    return [
        pltpu.VMEM((cols + 2 * edge, channels), F32),
        pltpu.VMEM((cols + 2 * edge - 8, channels), F32),
    ]


def kernel_grad(fields, left, right, grad, given, start):
    _, cols, channels = fields.shape
    count, edge, _ = left.shape
    taps = given.shape[0] - 1
    return pl.pallas_call(
        functools.partial(kernel_grad_kernel, start),
        in_specs=[resident()] * 5,
        out_specs=resident(),
        out_shape=resident_shape(taps + 1, channels),
        scratch_shapes=staging(cols, edge, channels) + [pltpu.VMEM((taps, 8, channels), F32)],
        compiler_params=pltpu.CompilerParams(vmem_limit_bytes=8 * 2**20),
        cost_estimate=pl.CostEstimate(
            flops=360 * taps * count * cols * channels, transcendentals=0,
            bytes_accessed=count * cols * channels * 8,
        ),
        name="kernel_grad",
    )(fields, left, right, grad, given)


def backward_kernel(start, grad_ref, left_ref, right_ref, cot_ref, kernel_ref, *refs):
    out_ref, s0, s4, kb = refs[-4:]
    _, cols, channels = grad_ref.shape
    rows, edge, _ = left_ref.shape
    base = start + pl.program_id(0) * rows
    taps = kernel_ref.shape[0]

    @pl.when(pl.program_id(0) == 0)
    def _():
        spread_taps(kb, kernel_ref, True)

    def one_row(r, carry):
        stage_row(s0, s4, left_ref[r], grad_ref[base + r], right_ref[r])
        for lane in lane_groups(channels):
            acc = conv_lane(s0, s4, kb, lane, cols, taps, edge)
            lanes = pl.ds(lane * 128, 128)
            back = jnp.concatenate(acc, axis=0) + cot_ref[r, :, lanes].astype(F32)
            out_ref[r, :, lanes] = back.astype(BF16)
        return carry

    lax.fori_loop(0, rows, one_row, 0)


def backward(grad, left, right, cot, kernel, carried, start):
    rows, cols, channels = grad.shape
    count, edge, _ = left.shape
    taps = kernel.shape[0]
    own = functools.partial(row_spec, BLOCK)
    at = pl.BlockSpec((BLOCK, cols, channels), lambda i: (i + start // BLOCK, 0, 0))
    return pl.pallas_call(
        functools.partial(backward_kernel, start),
        grid=(count // BLOCK,),
        in_specs=[resident(), own(edge, channels), own(edge, channels), at, resident()]
        + [pl.BlockSpec(memory_space=pl.ANY)] * len(carried),
        out_specs=at,
        out_shape=jax.ShapeDtypeStruct((rows, cols, channels), BF16),
        input_output_aliases={5: 0} if carried else {},
        scratch_shapes=staging(cols, edge, channels) + [pltpu.VMEM((taps, 8, channels), F32)],
        compiler_params=params(8),
        cost_estimate=pl.CostEstimate(
            flops=360 * taps * count * cols * channels, transcendentals=0,
            bytes_accessed=count * cols * channels * 10,
        ),
        name="backward",
    )(grad, left, right, cot, kernel, *carried)


def after(values, *others):
    held, _ = lax.optimization_barrier((values, others))
    return held


def chunk_starts(rows):
    half = rows // 2 // BLOCK * BLOCK
    return [0, half, rows]


def with_places(fields):
    found = groups()
    core = found[0][0][0]
    fields, places, index, even = lax.optimization_barrier(
        (fields, [places for places, _ in found], core.astype(jnp.int32).reshape(1), core == 0)
    )
    return fields, [(p, masks) for p, (_, masks) in zip(places, found)], index, even


def per_device(fields, cotangent, kernel, up_weight, down_weight):
    rows, cols, channels = fields.shape
    taps, hid = kernel.shape[0], up_weight.shape[1]
    edge = -(-KERNEL_SPACING * (taps // 2) // 8) * 8
    fields, (core, plane, depth), index, even = with_places(fields)
    bounds = chunk_starts(rows)
    chunks = list(zip(bounds[:-1], bounds[1:]))
    halos = []
    source, conv_inner = fields, None
    for begin, end in chunks:
        to_right, to_left = source[begin:end, cols - edge :], source[begin:end, :edge]
        halos.append((passed_along(to_right, 1), passed_along(to_left, -1)))
        if conv_inner is None:
            held = after(fields, to_right, to_left)
            conv_inner, up_t, down_t = inner(held, kernel, up_weight, down_weight)
            source = after(fields, conv_inner)
    carried = ()
    grad_halos = []
    for (begin, end), (left, right) in zip(chunks, halos):
        *carried, edge_left, edge_right = forward(
            index, conv_inner, left, right, fields, cotangent, kernel, up_weight, up_t, down_weight, down_t,
            carried, begin, end == rows,
        )
        if end < rows:
            grad_halos.append((passed_along(edge_right, 1), passed_along(edge_left, -1)))
    output, grad, mine, theirs = carried

    kgrad = jnp.zeros((taps + 1, channels), F32)

    def add_kernel_grad(total, which):
        left, right = halos[which]
        return kernel_grad(fields, left, right, grad, total, chunks[which][0])

    def add_field_grad(so_far, which):
        left, right = grad_halos[which]
        return (backward(grad, left, right, cotangent, kernel, so_far, chunks[which][0]),)

    theirs = after(theirs, grad_halos[0])
    part = mine + xor_permute(theirs, core[1][1]).astype(F32)
    sends, total = scatter_stage(part, plane)
    kgrad = after(kgrad, *sends)
    kgrad = add_kernel_grad(kgrad, 0)
    part = scatter_finish(sends, total, plane)
    part, edge_left, edge_right = lax.optimization_barrier((part, edge_left, edge_right))
    grad_halos.append((passed_along(edge_right, 1), passed_along(edge_left, -1)))
    sends, total = scatter_stage(part, depth)
    sends, kgrad = lax.optimization_barrier((sends, kgrad))
    kgrad = add_kernel_grad(kgrad, 1)
    part = scatter_finish(sends, total, depth).astype(BF16)
    packed = pack(part, kgrad)
    packed, halo = lax.optimization_barrier((packed, grad_halos[0]))
    grad_halos[0] = halo
    field_grad = add_field_grad((), 0)
    part, kgrad = gather_finish(packed, kgrad, depth)
    packed, field_grad, halo = lax.optimization_barrier((pack(part, kgrad), field_grad, grad_halos[1]))
    grad_halos[1] = halo
    field_grad = add_field_grad(field_grad, 1)
    part, kgrad = gather_finish(packed, kgrad, plane)
    packed = after(pack(part, kgrad), field_grad)
    got = xor_permute(packed, core[1][1])
    kgrad = kgrad + got[hid:].astype(F32)
    part = packed[:hid]
    factor = 1.0 / math.sqrt(rows * cols * lax.axis_size("lon") * lax.axis_size("lat"))
    got = got[:hid]
    gup = jnp.where(even, part, got).astype(F32) * factor
    gdown = jnp.where(even, got, part).astype(F32) * factor
    up_grad = gup.reshape(hid // 256, channels, 256).transpose(1, 0, 2).reshape(channels, hid)
    return (output, field_grad[0], kgrad[:taps] * factor, up_grad, gdown)


def solution(mesh):
    placed = (P("lat", "lon", None), P("lat", "lon", None), P(), P(), P())
    return jax.shard_map(
        per_device,
        mesh=mesh,
        in_specs=placed,
        out_specs=(P("lat", "lon", None), P("lat", "lon", None), P(), P(), P()),
        check_vma=False,
    )
```

```python
import functools
import math

import jax
import jax.numpy as jnp
from jax import lax
from jax.experimental import pallas as pl
from jax.experimental.pallas import tpu as pltpu
from jax.sharding import PartitionSpec as P

KERNEL_SPACING = 4
BLOCK = 8
NEAR_BLOCK = 16
FAR_BLOCK = 16
AXES = ("lon", "lat")
F32 = jnp.float32
BF16 = jnp.bfloat16
GELU_A = math.sqrt(2.0 / math.pi)
GELU_B = GELU_A * 0.044715


def xor_permute(value, mask):
    nlon, nlat = lax.axis_size("lon"), lax.axis_size("lat")
    lat_mask, lon_mask = mask
    pairs = [
        (lon * nlat + lat, (lon ^ lon_mask) * nlat + (lat ^ lat_mask))
        for lon in range(nlon)
        for lat in range(nlat)
    ]
    return lax.ppermute(value, AXES, pairs)


def on_chip(value):
    return xor_permute(value, (0, 1))


def off_chip(value):
    count = lax.axis_size("lon")
    pairs = [(i, (i + (1 if i % 2 else -1)) % count) for i in range(count)]
    return lax.ppermute(value, "lon", pairs)


def groups():
    nlon, nlat = lax.axis_size("lon"), lax.axis_size("lat")
    lon, lat = lax.axis_index("lon").astype(jnp.uint32), lax.axis_index("lat").astype(jnp.uint32)
    core = (lon & 1, [(0, s) for s in range(2)])
    plane = (lat * 2 + ((lon >> 1) & 1), [(s >> 1, (s & 1) * 2) for s in range(2 * nlat)])
    depth = (lon >> 2, [(0, s * 4) for s in range(nlon // 4)])
    return [([own ^ jnp.uint32(s) for s in range(len(masks))], masks) for own, masks in (core, plane, depth)]


def piece(parts, place):
    zero = jnp.uint32(0)
    return lax.dynamic_slice(parts, (place, zero, zero), (1,) + parts.shape[1:])[0]


def scatter_stage(value, group):
    places, _ = group
    size = len(places)
    parts = value.reshape(size, value.shape[0] // size, value.shape[1])
    return [piece(parts, p).astype(BF16) for p in places[1:]], piece(parts, places[0])


def scatter_finish(sends, total, group):
    _, masks = group
    for send, mask in zip(sends, masks[1:]):
        total = total + xor_permute(send, mask).astype(F32)
    return total


def gather_finish(packed, extra, group, beside):
    places, masks = group
    size = len(places)
    rows = packed.shape[0] - extra.shape[0]
    got = [packed[:rows]]
    parts, beside = lax.optimization_barrier(([xor_permute(packed, m) for m in masks[1:]], beside))
    for part in parts:
        got.append(part[:rows])
        extra = extra + part[rows:].astype(F32)
    whole = jnp.zeros((size, rows, packed.shape[1]), packed.dtype)
    zero = jnp.uint32(0)
    for part, place in zip(got, places):
        whole = lax.dynamic_update_slice(whole, part[None], (place, zero, zero))
    return whole.reshape(size * rows, packed.shape[1]), extra, beside


def pack(value, extra):
    return jnp.concatenate([value, extra.astype(BF16)], axis=0)


def lane_groups(channels):
    return range(channels // 128)


def halo_row(even, near, far):
    return jnp.where(even, far, near), jnp.where(even, near, far)


def stage_row(s0, s4, left, middle, right):
    edge, cols = left.shape[0], middle.shape[0]
    left, middle, right = left.astype(F32), middle.astype(F32), right.astype(F32)
    s0[pl.ds(0, edge), :] = left
    s0[pl.ds(edge, cols), :] = middle
    s0[pl.ds(edge + cols, edge), :] = right
    s4[pl.ds(0, edge - 4), :] = left[4:]
    s4[pl.ds(edge - 4, cols), :] = middle
    s4[pl.ds(edge - 4 + cols, edge - 4), :] = right[: edge - 4]


def spread_taps(kb, kernel_ref, flip):
    taps = kernel_ref.shape[0]
    for t in range(taps):
        row = kernel_ref[pl.ds(taps - 1 - t if flip else t, 1), :]
        kb[t] = jnp.broadcast_to(row, kb.shape[1:])


def tap_uses(blocks, taps, edge):
    lead = (edge - KERNEL_SPACING * (taps // 2)) // 4
    result = []
    for i in range(blocks + 2 * edge // 8):
        for half in (0, 1):
            uses = []
            for j in range(blocks):
                t = 2 * (i - j) + half - lead
                if 0 <= t < taps:
                    uses.append((j, t))
            if uses:
                result.append((i, half, uses))
    return result


def add_to(acc, at, term):
    acc[at] = term if acc[at] is None else acc[at] + term


def conv_lane(s0, s4, kb, lane, cols, taps, edge):
    lanes = pl.ds(lane * 128, 128)
    acc = [None] * (cols // 8)
    weights = [kb[t, :, lanes] for t in range(taps)]
    for i, half, uses in tap_uses(cols // 8, taps, edge):
        x = (s4 if half else s0)[pl.ds(8 * i, 8), lanes]
        for j, t in uses:
            add_to(acc, j, weights[t] * x)
    return acc


def row_spec(block, n, width):
    return pl.BlockSpec((block, n, width), lambda i: (i, 0, 0))


def whole_spec(*shape):
    return pl.BlockSpec(shape, lambda i: (0,) * len(shape))


def resident():
    return pl.BlockSpec(memory_space=pltpu.VMEM)


def resident_shape(*shape):
    return pltpu.VMEM(shape, F32)


def params(mib):
    return pltpu.CompilerParams(dimension_semantics=("arbitrary",), vmem_limit_bytes=mib * 2**20)


def halo_terms(edges, kb, lane, cols, taps, side):
    edge = edges.shape[1]
    lanes = pl.ds(lane * 128, 128)
    acc = {}
    for shifted in (0, 1):
        for i in range(edge // 8):
            column = ((-edge, 4 - edge), (cols, cols - 4))[side][shifted] + 8 * i
            x = None
            for j in range(cols // 8):
                t = (column - 8 * j) // 4 + taps // 2
                if 0 <= t < taps:
                    if x is None:
                        x = edges[shifted, pl.ds(8 * i, 8), lanes]
                    term = kb[t, :, lanes] * x
                    acc[j] = acc[j] + term if j in acc else term
    return acc


def stage_edges(edges, halo, side):
    edge = edges.shape[1]
    halo = halo.astype(F32)
    edges[0] = halo
    if side == 0:
        edges[1, pl.ds(0, edge - 4), :] = halo[4:]
    else:
        edges[1, pl.ds(4, edge - 4), :] = halo[: edge - 4]


def inner_kernel(
    core_ref, fields_ref, near_ref, kernel_ref, up_hbm, down_hbm, out_ref, upt_ref, downt_ref,
    s0, s4, kb, edges, up_ref, down_ref, sems,
):
    rows, cols, channels = fields_ref.shape
    taps = kernel_ref.shape[0]
    copies = [
        pltpu.make_async_copy(up_hbm, up_ref, sems.at[0]),
        pltpu.make_async_copy(down_hbm, down_ref, sems.at[1]),
    ]
    for copy in copies:
        copy.start()
    spread_taps(kb, kernel_ref, False)
    s4[...] = jnp.zeros_like(s4)
    edges[...] = jnp.zeros_like(edges)

    def one_row(side, r, carry):
        middle = fields_ref[r].astype(F32)
        s0[...] = middle
        s4[pl.ds(4, cols), :] = middle
        stage_edges(edges, near_ref[r], side)
        for lane in lane_groups(channels):
            lanes = pl.ds(lane * 128, 128)
            weights = [kb[t, :, lanes] for t in range(taps)]
            acc = [None] * (cols // 8)
            for i in range(cols // 8 + 1):
                for half, ref in ((0, s0), (1, s4)):
                    if half == 0 and i == cols // 8:
                        continue
                    x = ref[pl.ds(8 * i, 8), lanes]
                    for j in range(cols // 8):
                        t = 2 * (i - j) - half + taps // 2
                        if 0 <= t < taps:
                            add_to(acc, j, weights[t] * x)
            for j, value in halo_terms(edges, kb, lane, cols, taps, side).items():
                add_to(acc, j, value)
            for j, value in enumerate(acc):
                out_ref[r, pl.ds(8 * j, 8), lanes] = value
        return carry

    for side, here in ((1, core_ref[0] == 0), (0, core_ref[0] != 0)):

        @pl.when(here)
        def _(side=side):
            lax.fori_loop(0, rows, functools.partial(one_row, side), 0)

    for copy in copies:
        copy.wait()
    for j in range(up_ref.shape[1] // 256):
        part = pl.ds(256 * j, 256)
        upt_ref[part, :] = up_ref[:, part].T
        downt_ref[:, part] = down_ref[part, :].T


def inner(core, fields, near, kernel, up, down):
    rows, cols, channels = fields.shape
    taps, edge = kernel.shape[0], near.shape[1]
    return pl.pallas_call(
        inner_kernel,
        in_specs=[pl.BlockSpec(memory_space=pltpu.SMEM)]
        + [resident()] * 3
        + [pl.BlockSpec(memory_space=pltpu.HBM)] * 2,
        out_specs=[resident()] * 3,
        out_shape=[resident_shape(rows, cols, channels), pltpu.VMEM(down.shape, BF16), pltpu.VMEM(up.shape, BF16)],
        scratch_shapes=[
            pltpu.VMEM((cols, channels), F32),
            pltpu.VMEM((cols + 8, channels), F32),
            pltpu.VMEM((taps, 8, channels), F32),
            pltpu.VMEM((2, edge, channels), F32),
            pltpu.VMEM(up.shape, BF16),
            pltpu.VMEM(down.shape, BF16),
            pltpu.SemaphoreType.DMA((2,)),
        ],
        compiler_params=pltpu.CompilerParams(vmem_limit_bytes=8 * 2**20),
        cost_estimate=pl.CostEstimate(
            flops=260 * taps * rows * cols * channels, transcendentals=0,
            bytes_accessed=rows * cols * channels * 6,
        ),
        name="inner",
    )(core, fields, near, kernel, up, down)


def forward_kernel(
    reach, first, last, start, core_ref, inner_ref, far_ref, fields_ref, cot_ref, kernel_ref,
    up_ref, upt_ref, down_ref, downt_ref, *refs,
):
    given, refs = ((), refs) if first else (refs[2:4], refs[4:])
    (out_ref, grad_ref, gup_ref, gdt_ref), refs = refs[:4], refs[4:]
    if reach:
        (near_out_ref, far_out_ref), refs = refs[:2], refs[2:]
        edges, kb, conv_s = refs[:3]
        refs = refs[3:]
    normed_s, act_s, hg_s = refs[:3]
    gup_s, gdt_s = refs[3:] if last else (gup_ref, gdt_ref)
    step = pl.program_id(0)
    _, cols, channels = inner_ref.shape
    edge, taps = far_ref.shape[1], kernel_ref.shape[0]
    rows = FAR_BLOCK if reach else NEAR_BLOCK
    base_row = start + step * rows
    here = pl.ds(base_row, rows)
    even = core_ref[0] == 0
    hid = up_ref.shape[1]
    width = 256
    count = edge if reach else cols - edge
    cells = rows * count
    if reach:
        place = jnp.where(even, 0, cols - edge)
    else:
        place = jnp.where(even, edge, 0)
    span = pl.ds(pl.multiple_of(place, 16), count)

    @pl.when(step == 0)
    def _():
        if first:
            gup_s[...] = jnp.zeros_like(gup_s)
            gdt_s[...] = jnp.zeros_like(gdt_s)
        if last:
            gup_s[...] = given[0][...]
            gdt_s[...] = given[1][...]
        if reach:
            spread_taps(kb, kernel_ref, False)
            edges[...] = jnp.zeros_like(edges)

    if reach:

        def one_row(side, r, carry):
            stage_edges(edges, far_ref[r], side)
            for lane in lane_groups(channels):
                lanes = pl.ds(lane * 128, 128)
                terms = halo_terms(edges, kb, lane, cols, taps, side)
                skip = (cols - edge) // 8 if side else 0
                for j in range(count // 8):
                    base = inner_ref[base_row + r, pl.ds(8 * (j + skip), 8), lanes]
                    conv_s[r, pl.ds(8 * j, 8), lanes] = base + terms[j + skip] if j + skip in terms else base
            return carry

        for side, mine in ((0, even), (1, jnp.logical_not(even))):

            @pl.when(mine)
            def _(side=side):
                lax.fori_loop(0, rows, functools.partial(one_row, side), 0)

        conv = conv_s[...].reshape(cells, channels)
    else:
        conv = inner_ref[here, span, :].reshape(cells, channels)
    center = jnp.mean(conv, axis=-1, keepdims=True)
    deviation = conv - center
    spread = jnp.mean(deviation * deviation, axis=-1, keepdims=True)
    inv_scale = lax.rsqrt(spread + 1e-06)
    normed = deviation * inv_scale
    normed_s[...] = normed
    low = normed.astype(BF16)
    cot = cot_ref[here, span, :].reshape(cells, channels)
    over_cells = (((0,), (0,)), ((), ()))
    for j in range(hid // width):
        part = pl.ds(j * width, width)
        h = jnp.dot(low, up_ref[:, part], preferred_element_type=F32)
        u = jnp.dot(cot, downt_ref[:, part], preferred_element_type=F32)
        sq = h * h
        t = jnp.tanh(h * (GELU_A + GELU_B * sq))
        half = 0.5 * h
        act_s[:, part] = (half + half * t).astype(BF16)
        slope = (0.5 + 0.5 * t) + half * (1.0 - t * t) * (GELU_A + (3.0 * GELU_B) * sq)
        hg_s[:, part] = (u * slope).astype(BF16)
    out = jnp.dot(act_s[...], down_ref[...], preferred_element_type=F32)
    out = out + fields_ref[here, span, :].reshape(cells, channels).astype(F32)
    normed_grad = jnp.dot(hg_s[...], upt_ref[...], preferred_element_type=F32)
    for j in range(hid // width):
        part = pl.ds(j * width, width)
        gup_s[j] += lax.dot_general(low, hg_s[:, part], over_cells, preferred_element_type=F32)
        gdt_s[:, part] += lax.dot_general(cot, act_s[:, part], over_cells, preferred_element_type=F32)
    out_ref[here, span, :] = out.astype(BF16).reshape(rows, count, channels)
    normed = normed_s[...]
    mean_grad = jnp.mean(normed_grad, axis=-1, keepdims=True)
    mean_cross = jnp.mean(normed_grad * normed, axis=-1, keepdims=True)
    grad = inv_scale * (normed_grad - mean_grad - normed * mean_cross)
    grad = grad.reshape(rows, count, channels)
    grad_ref[here, span, :] = grad
    if reach:
        far_out_ref[...] = grad.astype(BF16)
        near_place = jnp.where(even, cols - edge, 0)
        near_out_ref[...] = grad_ref[here, pl.ds(pl.multiple_of(near_place, 16), edge), :].astype(BF16)

    if last:
        mine_ref, theirs_ref = gup_ref, gdt_ref
        ending = step == pl.num_programs(0) - 1

        @pl.when(ending & even)
        def _():
            for j in range(hid // width):
                part = pl.ds(j * width, width)
                mine_ref[part, :] = gup_s[j]
                theirs_ref[part, :] = gdt_s[:, part].T.astype(BF16)

        @pl.when(ending & jnp.logical_not(even))
        def _():
            for j in range(hid // width):
                part = pl.ds(j * width, width)
                theirs_ref[part, :] = gup_s[j].astype(BF16)
                mine_ref[part, :] = gdt_s[:, part].T


def forward(core, conv_inner, far, fields, cot, kernel, up, up_t, down, down_t, carried, reach, begin, end):
    rows, cols, channels = cot.shape
    edge = far.shape[1]
    taps, hid = kernel.shape[0], up.shape[1]
    count = edge if reach else cols - edge
    cells = (end - begin) * count
    last = reach and end == rows
    block = FAR_BLOCK if reach else NEAR_BLOCK
    own = row_spec(block, edge, channels)
    sums = [(hid // 256, channels, 256), (channels, hid)]
    ends = [((hid, channels), F32), ((hid, channels), BF16)] if last else [(s, F32) for s in sums]
    edges_out = [jax.ShapeDtypeStruct((end - begin, edge, channels), BF16)] * (2 if reach else 0)
    block_cells = block * count
    return pl.pallas_call(
        functools.partial(forward_kernel, reach, not carried, last, begin),
        grid=((end - begin) // block,),
        in_specs=[pl.BlockSpec(memory_space=pltpu.SMEM), resident(), own if reach else resident()]
        + [resident()] * (7 + len(carried)),
        out_specs=[resident()] * 4 + [own] * len(edges_out),
        out_shape=[pltpu.VMEM((rows, cols, channels), BF16), resident_shape(rows, cols, channels)]
        + [pltpu.VMEM(s, d) for s, d in ends]
        + edges_out,
        input_output_aliases={} if not carried else {10: 0, 11: 1} if last else {10: 0, 11: 1, 12: 2, 13: 3},
        scratch_shapes=(
            [
                pltpu.VMEM((2, edge, channels), F32),
                pltpu.VMEM((taps, 8, channels), F32),
                pltpu.VMEM((block, count, channels), F32),
            ]
            if reach
            else []
        )
        + [
            pltpu.VMEM((block_cells, channels), F32),
            pltpu.VMEM((block_cells, hid), BF16),
            pltpu.VMEM((block_cells, hid), BF16),
        ]
        + ([pltpu.VMEM(s, F32) for s in sums] if last else []),
        compiler_params=params(28),
        cost_estimate=pl.CostEstimate(
            flops=28 * cells * channels * hid, transcendentals=cells * hid,
            bytes_accessed=cells * channels * 12,
        ),
        name="forward",
    )(core, conv_inner, far, fields, cot, kernel, up, up_t, down, down_t, *carried)


def kernel_grad_kernel(start, core_ref, fields_ref, near_ref, far_ref, grad_ref, given_ref, out_ref, s0, s4, sums):
    _, cols, channels = fields_ref.shape
    rows, edge, _ = far_ref.shape
    even = core_ref[0] == 0
    taps = out_ref.shape[0] - 1
    blocks = cols // 8

    sums[...] = jnp.zeros_like(sums)

    def one_row(r, carry):
        left, right = halo_row(even, near_ref[start + r], far_ref[r])
        stage_row(s0, s4, left, fields_ref[start + r], right)
        for lane in lane_groups(channels):
            lanes = pl.ds(lane * 128, 128)
            grads = [grad_ref[start + r, pl.ds(8 * j, 8), lanes] for j in range(blocks)]
            acc = [None] * taps
            for i, half, uses in tap_uses(blocks, taps, edge):
                x = (s4 if half else s0)[pl.ds(8 * i, 8), lanes]
                for j, t in uses:
                    add_to(acc, t, grads[j] * x)
            for t in range(taps):
                sums[t, :, lanes] += acc[t]
        return carry

    lax.fori_loop(0, rows, one_row, 0)

    for t in range(taps):
        here = jnp.sum(sums[t], axis=0, keepdims=True)
        out_ref[pl.ds(t, 1), :] = given_ref[pl.ds(t, 1), :] + here
    out_ref[pl.ds(taps, 1), :] = jnp.zeros((1, channels), F32)


def staging(cols, edge, channels):
    return [
        pltpu.VMEM((cols + 2 * edge, channels), F32),
        pltpu.VMEM((cols + 2 * edge - 8, channels), F32),
    ]


def kernel_grad(core, fields, near, far, grad, given, start):
    _, cols, channels = fields.shape
    count, edge, _ = far.shape
    taps = given.shape[0] - 1
    return pl.pallas_call(
        functools.partial(kernel_grad_kernel, start),
        in_specs=[pl.BlockSpec(memory_space=pltpu.SMEM)] + [resident()] * 5,
        out_specs=resident(),
        out_shape=resident_shape(taps + 1, channels),
        scratch_shapes=staging(cols, edge, channels) + [pltpu.VMEM((taps, 8, channels), F32)],
        compiler_params=pltpu.CompilerParams(vmem_limit_bytes=8 * 2**20),
        cost_estimate=pl.CostEstimate(
            flops=360 * taps * count * cols * channels, transcendentals=0,
            bytes_accessed=count * cols * channels * 8,
        ),
        name="kernel_grad",
    )(core, fields, near, far, grad, given)


def backward_kernel(start, core_ref, grad_ref, near_ref, far_ref, cot_ref, kernel_ref, *refs):
    out_ref, s0, s4, kb = refs[-4:]
    _, cols, channels = grad_ref.shape
    rows, edge, _ = far_ref.shape
    even = core_ref[0] == 0
    base = start + pl.program_id(0) * rows
    taps = kernel_ref.shape[0]

    @pl.when(pl.program_id(0) == 0)
    def _():
        spread_taps(kb, kernel_ref, True)

    def one_row(r, carry):
        left, right = halo_row(even, near_ref[base + r], far_ref[r])
        stage_row(s0, s4, left, grad_ref[base + r], right)
        for lane in lane_groups(channels):
            acc = conv_lane(s0, s4, kb, lane, cols, taps, edge)
            lanes = pl.ds(lane * 128, 128)
            back = jnp.concatenate(acc, axis=0) + cot_ref[r, :, lanes].astype(F32)
            out_ref[r, :, lanes] = back.astype(BF16)
        return carry

    lax.fori_loop(0, rows, one_row, 0)


def backward(core, grad, near, far, cot, kernel, carried, start):
    rows, cols, channels = grad.shape
    count, edge, _ = far.shape
    taps = kernel.shape[0]
    own = functools.partial(row_spec, BLOCK)
    at = pl.BlockSpec((BLOCK, cols, channels), lambda i: (i + start // BLOCK, 0, 0))
    return pl.pallas_call(
        functools.partial(backward_kernel, start),
        grid=(count // BLOCK,),
        in_specs=[
            pl.BlockSpec(memory_space=pltpu.SMEM), resident(), resident(), own(edge, channels), at, resident(),
        ]
        + [pl.BlockSpec(memory_space=pl.ANY)] * len(carried),
        out_specs=at,
        out_shape=jax.ShapeDtypeStruct((rows, cols, channels), BF16),
        input_output_aliases={6: 0} if carried else {},
        scratch_shapes=staging(cols, edge, channels) + [pltpu.VMEM((taps, 8, channels), F32)],
        compiler_params=params(8),
        cost_estimate=pl.CostEstimate(
            flops=360 * taps * count * cols * channels, transcendentals=0,
            bytes_accessed=count * cols * channels * 10,
        ),
        name="backward",
    )(core, grad, near, far, cot, kernel, *carried)


def finish_kernel(factor, core_ref, own_ref, got_ref, tail_ref, kgrad_ref, up_ref, down_ref, taps_ref):
    even = core_ref[0] == 0
    own, got = own_ref[...].astype(F32) * factor, got_ref[...].astype(F32) * factor
    up_ref[...] = jnp.where(even, own, got)
    down_ref[...] = jnp.where(even, got, own)
    taps = taps_ref.shape[0]
    taps_ref[...] = (kgrad_ref[pl.ds(0, taps), :] + tail_ref[pl.ds(0, taps), :].astype(F32)) * factor


def finish(core, own, got, kgrad, taps, factor):
    hid, channels = own.shape[0] - kgrad.shape[0], own.shape[1]
    part = pl.BlockSpec((256, channels), lambda j: (j, 0))
    return pl.pallas_call(
        functools.partial(finish_kernel, factor),
        grid=(hid // 256,),
        in_specs=[
            pl.BlockSpec(memory_space=pltpu.SMEM), part, part,
            pl.BlockSpec(kgrad.shape, lambda j: (hid // kgrad.shape[0], 0)), whole_spec(*kgrad.shape),
        ],
        out_specs=[
            pl.BlockSpec((channels, 256), lambda j: (0, j)), part, whole_spec(taps, channels),
        ],
        out_shape=[
            jax.ShapeDtypeStruct((channels, hid), F32),
            jax.ShapeDtypeStruct((hid, channels), F32),
            jax.ShapeDtypeStruct((taps, channels), F32),
        ],
        compiler_params=params(8),
        name="finish",
    )(core, own, got, got, kgrad)


def after(values, *others):
    held, _ = lax.optimization_barrier((values, others))
    return held


def chunk_starts(rows):
    half = rows // 2 // BLOCK * BLOCK
    return [0, half, rows]


def with_places(fields):
    found = groups()
    core = found[0][0][0]
    fields, places, index, even = lax.optimization_barrier(
        (fields, [places for places, _ in found], core.astype(jnp.int32).reshape(1), core == 0)
    )
    return fields, [(p, masks) for p, (_, masks) in zip(places, found)], index, even


def per_device(fields, cotangent, kernel, up_weight, down_weight):
    rows, cols, channels = fields.shape
    taps, hid = kernel.shape[0], up_weight.shape[1]
    edge = -(-KERNEL_SPACING * (taps // 2) // 8) * 8
    fields, (core, plane, depth), index, even = with_places(fields)
    bounds = chunk_starts(rows)
    chunks = list(zip(bounds[:-1], bounds[1:]))
    to_left, to_right = fields[:, :edge], fields[:, cols - edge :]
    near_out, far_out = jnp.where(even, to_right, to_left), jnp.where(even, to_left, to_right)
    middle = chunks[0][1]
    near = on_chip(near_out)
    far = [off_chip(far_out[:middle])]
    near, _ = lax.optimization_barrier((near, far_out))
    conv_inner, up_t, down_t = inner(index, fields, near, kernel, up_weight, down_weight)
    far_out = after(far_out, conv_inner)
    far.append(off_chip(far_out[middle:]))

    def cells_of(carried, reach, halo, begin, end):
        return forward(
            index, conv_inner, halo, fields, cotangent, kernel, up_weight, up_t, down_weight, down_t,
            carried, reach, begin, end,
        )

    carried = cells_of((), False, near, 0, rows)
    grad_near, grad_far = [], []
    for (begin, end), arrived in zip(chunks, far):
        *carried, near_edge, far_edge = cells_of(carried, True, arrived, begin, end)
        grad_near.append(near_edge)
        if end < rows:
            grad_far.append(off_chip(far_edge))
    output, grad, mine, theirs = carried

    kgrad = jnp.zeros((taps + 1, channels), F32)

    def add_kernel_grad(total, which):
        return kernel_grad(index, fields, near, far[which], grad, total, chunks[which][0])

    def add_field_grad(so_far, which):
        return (
            backward(index, grad, grad_near, grad_far[which], cotangent, kernel, so_far, chunks[which][0]),
        )

    theirs = after(theirs, grad_far[0])
    part = mine + xor_permute(theirs, core[1][1]).astype(F32)
    sends, total = scatter_stage(part, plane)
    kgrad = after(kgrad, *sends)
    kgrad = add_kernel_grad(kgrad, 0)
    part = scatter_finish(sends, total, plane)
    part, far_edge = lax.optimization_barrier((part, far_edge))
    grad_far.append(off_chip(far_edge))
    grad_near = on_chip(jnp.concatenate(grad_near, axis=0))
    sends, total = scatter_stage(part, depth)
    sends, kgrad = lax.optimization_barrier((sends, kgrad))
    kgrad = add_kernel_grad(kgrad, 1)
    part = scatter_finish(sends, total, depth).astype(BF16)
    packed = pack(part, kgrad)
    packed, halo = lax.optimization_barrier((packed, grad_far[0]))
    grad_far[0] = halo
    field_grad = add_field_grad((), 0)
    part, kgrad, field_grad = gather_finish(packed, kgrad, depth, field_grad)
    packed, halo = lax.optimization_barrier((pack(part, kgrad), grad_far[1]))
    grad_far[1] = halo
    field_grad = add_field_grad(field_grad, 1)
    part, kgrad, field_grad = gather_finish(packed, kgrad, plane, field_grad)
    packed = pack(part, kgrad)
    got = on_chip(packed)
    factor = 1.0 / math.sqrt(rows * cols * lax.axis_size("lon") * lax.axis_size("lat"))
    up_grad, down_grad, tap_grad = finish(index, packed, got, kgrad, taps, factor)
    return (output, field_grad[0], tap_grad, up_grad, down_grad)


def solution(mesh):
    placed = (P("lat", "lon", None), P("lat", "lon", None), P(), P(), P())
    return jax.shard_map(
        per_device,
        mesh=mesh,
        in_specs=placed,
        out_specs=(P("lat", "lon", None), P("lat", "lon", None), P(), P(), P()),
        check_vma=False,
    )
```

```python
import functools
import math

import jax
import jax.numpy as jnp
from jax import lax
from jax.experimental import pallas as pl
from jax.experimental.pallas import tpu as pltpu
from jax.sharding import PartitionSpec as P

KERNEL_SPACING = 4
BLOCK = 4
NEAR_BLOCK = 16
FAR_BLOCK = 16
AXES = ("lon", "lat")
F32 = jnp.float32
BF16 = jnp.bfloat16
GELU_A = math.sqrt(2.0 / math.pi)
GELU_B = GELU_A * 0.044715


def xor_permute(value, mask):
    nlon, nlat = lax.axis_size("lon"), lax.axis_size("lat")
    lat_mask, lon_mask = mask
    pairs = [
        (lon * nlat + lat, (lon ^ lon_mask) * nlat + (lat ^ lat_mask))
        for lon in range(nlon)
        for lat in range(nlat)
    ]
    return lax.ppermute(value, AXES, pairs)


def on_chip(value):
    return xor_permute(value, (0, 1))


def off_chip(value):
    count = lax.axis_size("lon")
    pairs = [(i, (i + (1 if i % 2 else -1)) % count) for i in range(count)]
    return lax.ppermute(value, "lon", pairs)


def groups():
    nlon, nlat = lax.axis_size("lon"), lax.axis_size("lat")
    lon, lat = lax.axis_index("lon").astype(jnp.uint32), lax.axis_index("lat").astype(jnp.uint32)
    core = (lon & 1, [(0, s) for s in range(2)])
    plane = (lat * 2 + ((lon >> 1) & 1), [(s >> 1, (s & 1) * 2) for s in range(2 * nlat)])
    depth = (lon >> 2, [(0, s * 4) for s in range(nlon // 4)])
    return [([own ^ jnp.uint32(s) for s in range(len(masks))], masks) for own, masks in (core, plane, depth)]


def piece(parts, place):
    zero = jnp.uint32(0)
    return lax.dynamic_slice(parts, (place, zero, zero), (1,) + parts.shape[1:])[0]


def scatter_stage(value, group):
    places, _ = group
    size = len(places)
    parts = value.reshape(size, value.shape[0] // size, value.shape[1])
    return [piece(parts, p).astype(BF16) for p in places[1:]], piece(parts, places[0])


def scatter_finish(sends, total, group, beside):
    _, masks = group
    got, beside = lax.optimization_barrier(([xor_permute(v, m) for v, m in zip(sends, masks[1:])], beside))
    for part in got:
        total = total + part.astype(F32)
    return total, beside


def gather_finish(packed, extra, group, beside):
    places, masks = group
    size = len(places)
    rows = packed.shape[0] - extra.shape[0]
    got = [packed[:rows]]
    parts, beside = lax.optimization_barrier(([xor_permute(packed, m) for m in masks[1:]], beside))
    for part in parts:
        got.append(part[:rows])
        extra = extra + part[rows:].astype(F32)
    whole = jnp.zeros((size, rows, packed.shape[1]), packed.dtype)
    zero = jnp.uint32(0)
    for part, place in zip(got, places):
        whole = lax.dynamic_update_slice(whole, part[None], (place, zero, zero))
    return whole.reshape(size * rows, packed.shape[1]), extra, beside


def pack(value, extra):
    return jnp.concatenate([value, extra.astype(BF16)], axis=0)


def lane_groups(channels):
    return range(channels // 128)


def halo_row(even, near, far):
    return jnp.where(even, far, near), jnp.where(even, near, far)


def stage_row(s0, s4, left, middle, right):
    edge, cols = left.shape[0], middle.shape[0]
    left, middle, right = left.astype(F32), middle.astype(F32), right.astype(F32)
    s0[pl.ds(0, edge), :] = left
    s0[pl.ds(edge, cols), :] = middle
    s0[pl.ds(edge + cols, edge), :] = right
    s4[pl.ds(0, edge - 4), :] = left[4:]
    s4[pl.ds(edge - 4, cols), :] = middle
    s4[pl.ds(edge - 4 + cols, edge - 4), :] = right[: edge - 4]


def spread_taps(kb, kernel_ref, flip):
    taps = kernel_ref.shape[0]
    for t in range(taps):
        row = kernel_ref[pl.ds(taps - 1 - t if flip else t, 1), :]
        kb[t] = jnp.broadcast_to(row, kb.shape[1:])


def tap_uses(blocks, taps, edge):
    lead = (edge - KERNEL_SPACING * (taps // 2)) // 4
    result = []
    for i in range(blocks + 2 * edge // 8):
        for half in (0, 1):
            uses = []
            for j in range(blocks):
                t = 2 * (i - j) + half - lead
                if 0 <= t < taps:
                    uses.append((j, t))
            if uses:
                result.append((i, half, uses))
    return result


def add_to(acc, at, term):
    acc[at] = term if acc[at] is None else acc[at] + term


def conv_lane(s0, s4, kb, lane, cols, taps, edge):
    lanes = pl.ds(lane * 128, 128)
    acc = [None] * (cols // 8)
    weights = [kb[t, :, lanes] for t in range(taps)]
    for i, half, uses in tap_uses(cols // 8, taps, edge):
        x = (s4 if half else s0)[pl.ds(8 * i, 8), lanes]
        for j, t in uses:
            add_to(acc, j, weights[t] * x)
    return acc


def row_spec(block, n, width):
    return pl.BlockSpec((block, n, width), lambda i: (i, 0, 0))


def whole_spec(*shape):
    return pl.BlockSpec(shape, lambda i: (0,) * len(shape))


def resident():
    return pl.BlockSpec(memory_space=pltpu.VMEM)


def resident_shape(*shape):
    return pltpu.VMEM(shape, F32)


def params(mib):
    return pltpu.CompilerParams(dimension_semantics=("arbitrary",), vmem_limit_bytes=mib * 2**20)


def halo_terms(edges, kb, lane, cols, taps, side):
    edge = edges.shape[1]
    lanes = pl.ds(lane * 128, 128)
    acc = {}
    for shifted in (0, 1):
        for i in range(edge // 8):
            column = ((-edge, 4 - edge), (cols, cols - 4))[side][shifted] + 8 * i
            x = None
            for j in range(cols // 8):
                t = (column - 8 * j) // 4 + taps // 2
                if 0 <= t < taps:
                    if x is None:
                        x = edges[shifted, pl.ds(8 * i, 8), lanes]
                    term = kb[t, :, lanes] * x
                    acc[j] = acc[j] + term if j in acc else term
    return acc


def stage_edges(edges, halo, side):
    edge = edges.shape[1]
    halo = halo.astype(F32)
    edges[0] = halo
    if side == 0:
        edges[1, pl.ds(0, edge - 4), :] = halo[4:]
    else:
        edges[1, pl.ds(4, edge - 4), :] = halo[: edge - 4]


def inner_kernel(
    core_ref, fields_ref, near_ref, kernel_ref, up_hbm, down_hbm, out_ref, upt_ref, downt_ref,
    s0, s4, kb, edges, up_ref, down_ref, sems,
):
    rows, cols, channels = fields_ref.shape
    taps = kernel_ref.shape[0]
    copies = [
        pltpu.make_async_copy(up_hbm, up_ref, sems.at[0]),
        pltpu.make_async_copy(down_hbm, down_ref, sems.at[1]),
    ]
    for copy in copies:
        copy.start()
    spread_taps(kb, kernel_ref, False)
    s4[...] = jnp.zeros_like(s4)
    edges[...] = jnp.zeros_like(edges)

    def one_row(side, r, carry):
        middle = fields_ref[r].astype(F32)
        s0[...] = middle
        s4[pl.ds(4, cols), :] = middle
        stage_edges(edges, near_ref[r], side)
        for lane in lane_groups(channels):
            lanes = pl.ds(lane * 128, 128)
            weights = [kb[t, :, lanes] for t in range(taps)]
            acc = [None] * (cols // 8)
            for i in range(cols // 8 + 1):
                for half, ref in ((0, s0), (1, s4)):
                    if half == 0 and i == cols // 8:
                        continue
                    x = ref[pl.ds(8 * i, 8), lanes]
                    for j in range(cols // 8):
                        t = 2 * (i - j) - half + taps // 2
                        if 0 <= t < taps:
                            add_to(acc, j, weights[t] * x)
            for j, value in halo_terms(edges, kb, lane, cols, taps, side).items():
                add_to(acc, j, value)
            for j, value in enumerate(acc):
                out_ref[r, pl.ds(8 * j, 8), lanes] = value
        return carry

    for side, here in ((1, core_ref[0] == 0), (0, core_ref[0] != 0)):

        @pl.when(here)
        def _(side=side):
            lax.fori_loop(0, rows, functools.partial(one_row, side), 0)

    for copy in copies:
        copy.wait()
    for j in range(up_ref.shape[1] // 256):
        part = pl.ds(256 * j, 256)
        upt_ref[part, :] = up_ref[:, part].T
        downt_ref[:, part] = down_ref[part, :].T


def inner(core, fields, near, kernel, up, down):
    rows, cols, channels = fields.shape
    taps, edge = kernel.shape[0], near.shape[1]
    return pl.pallas_call(
        inner_kernel,
        in_specs=[pl.BlockSpec(memory_space=pltpu.SMEM)]
        + [resident()] * 3
        + [pl.BlockSpec(memory_space=pltpu.HBM)] * 2,
        out_specs=[resident()] * 3,
        out_shape=[resident_shape(rows, cols, channels), pltpu.VMEM(down.shape, BF16), pltpu.VMEM(up.shape, BF16)],
        scratch_shapes=[
            pltpu.VMEM((cols, channels), F32),
            pltpu.VMEM((cols + 8, channels), F32),
            pltpu.VMEM((taps, 8, channels), F32),
            pltpu.VMEM((2, edge, channels), F32),
            pltpu.VMEM(up.shape, BF16),
            pltpu.VMEM(down.shape, BF16),
            pltpu.SemaphoreType.DMA((2,)),
        ],
        compiler_params=pltpu.CompilerParams(vmem_limit_bytes=8 * 2**20),
        cost_estimate=pl.CostEstimate(
            flops=260 * taps * rows * cols * channels, transcendentals=0,
            bytes_accessed=rows * cols * channels * 6,
        ),
        name="inner",
    )(core, fields, near, kernel, up, down)


def forward_kernel(
    reach, first, last, start, core_ref, inner_ref, far_ref, fields_ref, cot_ref, kernel_ref,
    up_ref, upt_ref, down_ref, downt_ref, *refs,
):
    given, refs = ((), refs) if first else (refs[2:4], refs[4:])
    (out_ref, grad_ref, gup_ref, gdt_ref), refs = refs[:4], refs[4:]
    if reach:
        (near_out_ref, far_out_ref), refs = refs[:2], refs[2:]
        edges, kb, conv_s = refs[:3]
        refs = refs[3:]
    normed_s, act_s, hg_s = refs[:3]
    gup_s, gdt_s = refs[3:] if last else (gup_ref, gdt_ref)
    step = pl.program_id(0)
    _, cols, channels = inner_ref.shape
    edge, taps = far_ref.shape[1], kernel_ref.shape[0]
    rows = far_ref.shape[0] if reach else NEAR_BLOCK
    base_row = start + step * rows
    here = pl.ds(base_row, rows)
    even = core_ref[0] == 0
    hid = up_ref.shape[1]
    width = 256
    count = edge if reach else cols - edge
    cells = rows * count
    if reach:
        place = jnp.where(even, 0, cols - edge)
    else:
        place = jnp.where(even, edge, 0)
    span = pl.ds(pl.multiple_of(place, 16), count)

    @pl.when(step == 0)
    def _():
        if first:
            gup_s[...] = jnp.zeros_like(gup_s)
            gdt_s[...] = jnp.zeros_like(gdt_s)
        if last:
            gup_s[...] = given[0][...]
            gdt_s[...] = given[1][...]
        if reach:
            spread_taps(kb, kernel_ref, False)
            edges[...] = jnp.zeros_like(edges)

    if reach:

        def one_row(side, r, carry):
            stage_edges(edges, far_ref[r], side)
            for lane in lane_groups(channels):
                lanes = pl.ds(lane * 128, 128)
                terms = halo_terms(edges, kb, lane, cols, taps, side)
                skip = (cols - edge) // 8 if side else 0
                for j in range(count // 8):
                    base = inner_ref[base_row + r, pl.ds(8 * (j + skip), 8), lanes]
                    conv_s[r, pl.ds(8 * j, 8), lanes] = base + terms[j + skip] if j + skip in terms else base
            return carry

        for side, mine in ((0, even), (1, jnp.logical_not(even))):

            @pl.when(mine)
            def _(side=side):
                lax.fori_loop(0, rows, functools.partial(one_row, side), 0)

        conv = conv_s[...].reshape(cells, channels)
    else:
        conv = inner_ref[here, span, :].reshape(cells, channels)
    center = jnp.mean(conv, axis=-1, keepdims=True)
    deviation = conv - center
    spread = jnp.mean(deviation * deviation, axis=-1, keepdims=True)
    inv_scale = lax.rsqrt(spread + 1e-06)
    normed = deviation * inv_scale
    normed_s[...] = normed
    low = normed.astype(BF16)
    cot = cot_ref[here, span, :].reshape(cells, channels)
    over_cells = (((0,), (0,)), ((), ()))
    for j in range(hid // width):
        part = pl.ds(j * width, width)
        h = jnp.dot(low, up_ref[:, part], preferred_element_type=F32)
        u = jnp.dot(cot, downt_ref[:, part], preferred_element_type=F32)
        sq = h * h
        t = jnp.tanh(h * (GELU_A + GELU_B * sq))
        half = 0.5 * h
        act_s[:, part] = (half + half * t).astype(BF16)
        slope = (0.5 + 0.5 * t) + half * (1.0 - t * t) * (GELU_A + (3.0 * GELU_B) * sq)
        hg_s[:, part] = (u * slope).astype(BF16)
    out = jnp.dot(act_s[...], down_ref[...], preferred_element_type=F32)
    out = out + fields_ref[here, span, :].reshape(cells, channels).astype(F32)
    normed_grad = jnp.dot(hg_s[...], upt_ref[...], preferred_element_type=F32)
    for j in range(hid // width):
        part = pl.ds(j * width, width)
        gup_s[j] += lax.dot_general(low, hg_s[:, part], over_cells, preferred_element_type=F32)
        gdt_s[:, part] += lax.dot_general(cot, act_s[:, part], over_cells, preferred_element_type=F32)
    out_ref[here, span, :] = out.astype(BF16).reshape(rows, count, channels)
    normed = normed_s[...]
    mean_grad = jnp.mean(normed_grad, axis=-1, keepdims=True)
    mean_cross = jnp.mean(normed_grad * normed, axis=-1, keepdims=True)
    grad = inv_scale * (normed_grad - mean_grad - normed * mean_cross)
    grad = grad.reshape(rows, count, channels)
    grad_ref[here, span, :] = grad
    if reach:
        far_out_ref[...] = grad.astype(BF16)
        near_place = jnp.where(even, cols - edge, 0)
        near_out_ref[...] = grad_ref[here, pl.ds(pl.multiple_of(near_place, 16), edge), :].astype(BF16)

    if last:
        mine_ref, theirs_ref = gup_ref, gdt_ref
        ending = step == pl.num_programs(0) - 1

        @pl.when(ending & even)
        def _():
            for j in range(hid // width):
                part = pl.ds(j * width, width)
                mine_ref[part, :] = gup_s[j]
                theirs_ref[part, :] = gdt_s[:, part].T.astype(BF16)

        @pl.when(ending & jnp.logical_not(even))
        def _():
            for j in range(hid // width):
                part = pl.ds(j * width, width)
                theirs_ref[part, :] = gup_s[j].astype(BF16)
                mine_ref[part, :] = gdt_s[:, part].T


def forward(core, conv_inner, far, fields, cot, kernel, up, up_t, down, down_t, carried, reach, begin, end):
    rows, cols, channels = cot.shape
    edge = far.shape[1]
    taps, hid = kernel.shape[0], up.shape[1]
    count = edge if reach else cols - edge
    cells = (end - begin) * count
    last = reach and end == rows
    block = end - begin if reach else NEAR_BLOCK
    own = row_spec(block, edge, channels)
    sums = [(hid // 256, channels, 256), (channels, hid)]
    ends = [((hid, channels), F32), ((hid, channels), BF16)] if last else [(s, F32) for s in sums]
    edges_out = [jax.ShapeDtypeStruct((end - begin, edge, channels), BF16)] * (2 if reach else 0)
    block_cells = block * count
    return pl.pallas_call(
        functools.partial(forward_kernel, reach, not carried, last, begin),
        grid=((end - begin) // block,),
        in_specs=[pl.BlockSpec(memory_space=pltpu.SMEM), resident(), own if reach else resident()]
        + [resident()] * (7 + len(carried)),
        out_specs=[resident()] * 4 + [own] * len(edges_out),
        out_shape=[pltpu.VMEM((rows, cols, channels), BF16), resident_shape(rows, cols, channels)]
        + [pltpu.VMEM(s, d) for s, d in ends]
        + edges_out,
        input_output_aliases={} if not carried else {10: 0, 11: 1} if last else {10: 0, 11: 1, 12: 2, 13: 3},
        scratch_shapes=(
            [
                pltpu.VMEM((2, edge, channels), F32),
                pltpu.VMEM((taps, 8, channels), F32),
                pltpu.VMEM((block, count, channels), F32),
            ]
            if reach
            else []
        )
        + [
            pltpu.VMEM((block_cells, channels), F32),
            pltpu.VMEM((block_cells, hid), BF16),
            pltpu.VMEM((block_cells, hid), BF16),
        ]
        + ([pltpu.VMEM(s, F32) for s in sums] if last else []),
        compiler_params=params(28),
        cost_estimate=pl.CostEstimate(
            flops=28 * cells * channels * hid, transcendentals=cells * hid,
            bytes_accessed=cells * channels * 12,
        ),
        name="forward",
    )(core, conv_inner, far, fields, cot, kernel, up, up_t, down, down_t, *carried)


def kernel_grad_kernel(start, core_ref, fields_ref, near_ref, far_ref, grad_ref, given_ref, out_ref, s0, s4, sums):
    _, cols, channels = fields_ref.shape
    rows, edge, _ = far_ref.shape
    even = core_ref[0] == 0
    taps = out_ref.shape[0] - 1
    blocks = cols // 8

    sums[...] = jnp.zeros_like(sums)

    def one_row(r, carry):
        left, right = halo_row(even, near_ref[start + r], far_ref[r])
        stage_row(s0, s4, left, fields_ref[start + r], right)
        for lane in lane_groups(channels):
            lanes = pl.ds(lane * 128, 128)
            grads = [grad_ref[start + r, pl.ds(8 * j, 8), lanes] for j in range(blocks)]
            acc = [None] * taps
            for i, half, uses in tap_uses(blocks, taps, edge):
                x = (s4 if half else s0)[pl.ds(8 * i, 8), lanes]
                for j, t in uses:
                    add_to(acc, t, grads[j] * x)
            for t in range(taps):
                sums[t, :, lanes] += acc[t]
        return carry

    lax.fori_loop(0, rows, one_row, 0)

    for t in range(taps):
        here = jnp.sum(sums[t], axis=0, keepdims=True)
        out_ref[pl.ds(t, 1), :] = given_ref[pl.ds(t, 1), :] + here
    out_ref[pl.ds(taps, 1), :] = jnp.zeros((1, channels), F32)


def staging(cols, edge, channels):
    return [
        pltpu.VMEM((cols + 2 * edge, channels), F32),
        pltpu.VMEM((cols + 2 * edge - 8, channels), F32),
    ]


def kernel_grad(core, fields, near, far, grad, given, start):
    _, cols, channels = fields.shape
    count, edge, _ = far.shape
    taps = given.shape[0] - 1
    return pl.pallas_call(
        functools.partial(kernel_grad_kernel, start),
        in_specs=[pl.BlockSpec(memory_space=pltpu.SMEM)] + [resident()] * 5,
        out_specs=resident(),
        out_shape=resident_shape(taps + 1, channels),
        scratch_shapes=staging(cols, edge, channels) + [pltpu.VMEM((taps, 8, channels), F32)],
        compiler_params=pltpu.CompilerParams(vmem_limit_bytes=8 * 2**20),
        cost_estimate=pl.CostEstimate(
            flops=60 * taps * count * cols * channels, transcendentals=0,
            bytes_accessed=count * cols * channels * 8,
        ),
        name="kernel_grad",
    )(core, fields, near, far, grad, given)


def backward_kernel(start, core_ref, grad_ref, near_ref, far_ref, cot_ref, kernel_ref, *refs):
    out_ref, s0, s4, kb = refs[-4:]
    _, cols, channels = grad_ref.shape
    rows, edge, _ = far_ref.shape
    even = core_ref[0] == 0
    base = start + pl.program_id(0) * rows
    taps = kernel_ref.shape[0]

    @pl.when(pl.program_id(0) == 0)
    def _():
        spread_taps(kb, kernel_ref, True)

    def one_row(r, carry):
        left, right = halo_row(even, near_ref[base + r], far_ref[r])
        stage_row(s0, s4, left, grad_ref[base + r], right)
        for lane in lane_groups(channels):
            acc = conv_lane(s0, s4, kb, lane, cols, taps, edge)
            lanes = pl.ds(lane * 128, 128)
            back = jnp.concatenate(acc, axis=0) + cot_ref[r, :, lanes].astype(F32)
            out_ref[r, :, lanes] = back.astype(BF16)
        return carry

    lax.fori_loop(0, rows, one_row, 0)


def backward(core, grad, near, far, cot, kernel, carried, start):
    rows, cols, channels = grad.shape
    count, edge, _ = far.shape
    taps = kernel.shape[0]
    own = functools.partial(row_spec, BLOCK)
    at = pl.BlockSpec((BLOCK, cols, channels), lambda i: (i + start // BLOCK, 0, 0))
    return pl.pallas_call(
        functools.partial(backward_kernel, start),
        grid=(count // BLOCK,),
        in_specs=[
            pl.BlockSpec(memory_space=pltpu.SMEM), resident(), resident(), own(edge, channels), at, resident(),
        ]
        + [pl.BlockSpec(memory_space=pl.ANY)] * len(carried),
        out_specs=at,
        out_shape=jax.ShapeDtypeStruct((rows, cols, channels), BF16),
        input_output_aliases={6: 0} if carried else {},
        scratch_shapes=staging(cols, edge, channels) + [pltpu.VMEM((taps, 8, channels), F32)],
        compiler_params=params(8),
        cost_estimate=pl.CostEstimate(
            flops=60 * taps * count * cols * channels, transcendentals=0,
            bytes_accessed=count * cols * channels * 10,
        ),
        name="backward",
    )(core, grad, near, far, cot, kernel, *carried)


def finish_kernel(factor, core_ref, own_ref, got_ref, tail_ref, kgrad_ref, up_ref, down_ref, taps_ref):
    even = core_ref[0] == 0
    own, got = own_ref[...].astype(F32) * factor, got_ref[...].astype(F32) * factor
    up_ref[...] = jnp.where(even, own, got)
    down_ref[...] = jnp.where(even, got, own)
    taps = taps_ref.shape[0]
    taps_ref[...] = (kgrad_ref[pl.ds(0, taps), :] + tail_ref[pl.ds(0, taps), :].astype(F32)) * factor


def finish(core, own, got, kgrad, taps, factor):
    hid, channels = own.shape[0] - kgrad.shape[0], own.shape[1]
    part = pl.BlockSpec((256, channels), lambda j: (j, 0))
    return pl.pallas_call(
        functools.partial(finish_kernel, factor),
        grid=(hid // 256,),
        in_specs=[
            pl.BlockSpec(memory_space=pltpu.SMEM), part, part,
            pl.BlockSpec(kgrad.shape, lambda j: (hid // kgrad.shape[0], 0)), whole_spec(*kgrad.shape),
        ],
        out_specs=[
            pl.BlockSpec((channels, 256), lambda j: (0, j)), part, whole_spec(taps, channels),
        ],
        out_shape=[
            jax.ShapeDtypeStruct((channels, hid), F32),
            jax.ShapeDtypeStruct((hid, channels), F32),
            jax.ShapeDtypeStruct((taps, channels), F32),
        ],
        compiler_params=params(8),
        name="finish",
    )(core, own, got, got, kgrad)


def after(values, *others):
    held, _ = lax.optimization_barrier((values, others))
    return held


def chunk_starts(rows):
    first = rows * 3 // 8 // BLOCK * BLOCK
    return [0, first, rows]


def with_places(fields):
    found = groups()
    core = found[0][0][0]
    fields, places, index, even = lax.optimization_barrier(
        (fields, [places for places, _ in found], core.astype(jnp.int32).reshape(1), core == 0)
    )
    return fields, [(p, masks) for p, (_, masks) in zip(places, found)], index, even


def per_device(fields, cotangent, kernel, up_weight, down_weight):
    rows, cols, channels = fields.shape
    taps, hid = kernel.shape[0], up_weight.shape[1]
    edge = -(-KERNEL_SPACING * (taps // 2) // 8) * 8
    fields, (core, plane, depth), index, even = with_places(fields)
    bounds = chunk_starts(rows)
    chunks = list(zip(bounds[:-1], bounds[1:]))
    to_left, to_right = fields[:, :edge], fields[:, cols - edge :]
    near_out, far_out = jnp.where(even, to_right, to_left), jnp.where(even, to_left, to_right)
    middle = chunks[0][1]
    near = on_chip(near_out)
    far = [off_chip(far_out[:middle])]
    near, _ = lax.optimization_barrier((near, far_out))
    conv_inner, up_t, down_t = inner(index, fields, near, kernel, up_weight, down_weight)
    far_out = after(far_out, conv_inner)
    far.append(off_chip(far_out[middle:]))

    def cells_of(carried, reach, halo, begin, end):
        return forward(
            index, conv_inner, halo, fields, cotangent, kernel, up_weight, up_t, down_weight, down_t,
            carried, reach, begin, end,
        )

    carried = cells_of((), False, near, 0, rows)
    grad_near, grad_far = [], []
    for (begin, end), arrived in zip(chunks, far):
        *carried, near_edge, far_edge = cells_of(carried, True, arrived, begin, end)
        grad_near.append(near_edge)
        if end < rows:
            grad_far.append(off_chip(far_edge))
    output, grad, mine, theirs = carried

    kgrad = jnp.zeros((taps + 1, channels), F32)

    def add_kernel_grad(total, which):
        return kernel_grad(index, fields, near, far[which], grad, total, chunks[which][0])

    def add_field_grad(so_far, which):
        return (
            backward(index, grad, grad_near, grad_far[which], cotangent, kernel, so_far, chunks[which][0]),
        )

    theirs = after(theirs, grad_far[0])
    part = mine + xor_permute(theirs, core[1][1]).astype(F32)
    sends, total = scatter_stage(part, plane)
    kgrad = after(kgrad, *sends)
    kgrad = add_kernel_grad(kgrad, 0)
    part, kgrad = scatter_finish(sends, total, plane, kgrad)
    part, far_edge = lax.optimization_barrier((part, far_edge))
    grad_far.append(off_chip(far_edge))
    grad_near = on_chip(jnp.concatenate(grad_near, axis=0))
    sends, total = scatter_stage(part, depth)
    sends, kgrad = lax.optimization_barrier((sends, kgrad))
    kgrad = add_kernel_grad(kgrad, 1)
    part, kgrad = scatter_finish(sends, total, depth, kgrad)
    part = part.astype(BF16)
    packed = pack(part, kgrad)
    grad_far, _ = lax.optimization_barrier((grad_far, packed))
    field_grad = add_field_grad((), 0)
    part, kgrad, field_grad = gather_finish(packed, kgrad, depth, field_grad)
    packed = pack(part, kgrad)
    field_grad, grad_far[1] = lax.optimization_barrier((field_grad, after(grad_far[1], packed)))
    field_grad = add_field_grad(field_grad, 1)
    part, kgrad, field_grad = gather_finish(packed, kgrad, plane, field_grad)
    packed = pack(part, kgrad)
    got = on_chip(packed)
    factor = 1.0 / math.sqrt(rows * cols * lax.axis_size("lon") * lax.axis_size("lat"))
    up_grad, down_grad, tap_grad = finish(index, packed, got, kgrad, taps, factor)
    return (output, field_grad[0], tap_grad, up_grad, down_grad)


def solution(mesh):
    placed = (P("lat", "lon", None), P("lat", "lon", None), P(), P(), P())
    return jax.shard_map(
        per_device,
        mesh=mesh,
        in_specs=placed,
        out_specs=(P("lat", "lon", None), P("lat", "lon", None), P(), P(), P()),
        check_vma=False,
    )
```

```python
import functools
import math

import jax
import jax.numpy as jnp
from jax import lax
from jax.experimental import pallas as pl
from jax.experimental.pallas import tpu as pltpu
from jax.sharding import PartitionSpec as P

KERNEL_SPACING = 4
BLOCK = 4
NEAR_BLOCK = 16
FAR_BLOCK = 16
AXES = ("lon", "lat")
F32 = jnp.float32
BF16 = jnp.bfloat16
GELU_A = math.sqrt(2.0 / math.pi)
GELU_B = GELU_A * 0.044715


def xor_permute(value, mask):
    nlon, nlat = lax.axis_size("lon"), lax.axis_size("lat")
    lat_mask, lon_mask = mask
    pairs = [
        (lon * nlat + lat, (lon ^ lon_mask) * nlat + (lat ^ lat_mask))
        for lon in range(nlon)
        for lat in range(nlat)
    ]
    return lax.ppermute(value, AXES, pairs)


def on_chip(value):
    return xor_permute(value, (0, 1))


def off_chip(value):
    count = lax.axis_size("lon")
    pairs = [(i, (i + (1 if i % 2 else -1)) % count) for i in range(count)]
    return lax.ppermute(value, "lon", pairs)


def groups():
    nlon, nlat = lax.axis_size("lon"), lax.axis_size("lat")
    lon, lat = lax.axis_index("lon").astype(jnp.uint32), lax.axis_index("lat").astype(jnp.uint32)
    core = (lon & 1, [(0, s) for s in range(2)])
    plane = (lat * 2 + ((lon >> 1) & 1), [(s >> 1, (s & 1) * 2) for s in range(2 * nlat)])
    depth = (lon >> 2, [(0, s * 4) for s in range(nlon // 4)])
    return [([own ^ jnp.uint32(s) for s in range(len(masks))], masks) for own, masks in (core, plane, depth)]


def piece(parts, place):
    zero = jnp.uint32(0)
    return lax.dynamic_slice(parts, (place, zero, zero), (1,) + parts.shape[1:])[0]


def scatter_stage(value, group):
    places, _ = group
    size = len(places)
    parts = value.reshape(size, value.shape[0] // size, value.shape[1])
    return [piece(parts, p).astype(BF16) for p in places[1:]], piece(parts, places[0])


def scatter_finish(sends, total, group, beside):
    _, masks = group
    got, beside = lax.optimization_barrier(([xor_permute(v, m) for v, m in zip(sends, masks[1:])], beside))
    for part in got:
        total = total + part.astype(F32)
    return total, beside


def gather_finish(packed, extra, group, beside):
    places, masks = group
    size = len(places)
    rows = packed.shape[0] - extra.shape[0]
    got = [packed[:rows]]
    parts, beside = lax.optimization_barrier(([xor_permute(packed, m) for m in masks[1:]], beside))
    for part in parts:
        got.append(part[:rows])
        extra = extra + part[rows:].astype(F32)
    whole = jnp.zeros((size, rows, packed.shape[1]), packed.dtype)
    zero = jnp.uint32(0)
    for part, place in zip(got, places):
        whole = lax.dynamic_update_slice(whole, part[None], (place, zero, zero))
    return whole.reshape(size * rows, packed.shape[1]), extra, beside


def pack(value, extra):
    return jnp.concatenate([value, extra.astype(BF16)], axis=0)


def lane_groups(channels):
    return range(channels // 128)


def halo_row(even, near, far):
    return jnp.where(even, far, near), jnp.where(even, near, far)


def stage_row(s0, s4, left, middle, right):
    edge, cols = left.shape[0], middle.shape[0]
    left, middle, right = left.astype(F32), middle.astype(F32), right.astype(F32)
    s0[pl.ds(0, edge), :] = left
    s0[pl.ds(edge, cols), :] = middle
    s0[pl.ds(edge + cols, edge), :] = right
    s4[pl.ds(0, edge - 4), :] = left[4:]
    s4[pl.ds(edge - 4, cols), :] = middle
    s4[pl.ds(edge - 4 + cols, edge - 4), :] = right[: edge - 4]


def spread_taps(kb, kernel_ref, flip):
    taps = kernel_ref.shape[0]
    for t in range(taps):
        row = kernel_ref[pl.ds(taps - 1 - t if flip else t, 1), :]
        kb[t] = jnp.broadcast_to(row, kb.shape[1:])


def tap_uses(blocks, taps, edge):
    lead = (edge - KERNEL_SPACING * (taps // 2)) // 4
    result = []
    for i in range(blocks + 2 * edge // 8):
        for half in (0, 1):
            uses = []
            for j in range(blocks):
                t = 2 * (i - j) + half - lead
                if 0 <= t < taps:
                    uses.append((j, t))
            if uses:
                result.append((i, half, uses))
    return result


def add_to(acc, at, term):
    acc[at] = term if acc[at] is None else acc[at] + term


def conv_lane(s0, s4, kb, lane, cols, taps, edge):
    lanes = pl.ds(lane * 128, 128)
    acc = [None] * (cols // 8)
    weights = [kb[t, :, lanes] for t in range(taps)]
    for i, half, uses in tap_uses(cols // 8, taps, edge):
        x = (s4 if half else s0)[pl.ds(8 * i, 8), lanes]
        for j, t in uses:
            add_to(acc, j, weights[t] * x)
    return acc


def row_spec(block, n, width):
    return pl.BlockSpec((block, n, width), lambda i: (i, 0, 0))


def whole_spec(*shape):
    return pl.BlockSpec(shape, lambda i: (0,) * len(shape))


def resident():
    return pl.BlockSpec(memory_space=pltpu.VMEM)


def resident_shape(*shape):
    return pltpu.VMEM(shape, F32)


def params(mib):
    return pltpu.CompilerParams(dimension_semantics=("arbitrary",), vmem_limit_bytes=mib * 2**20)


def halo_terms(edges, kb, lane, cols, taps, side):
    edge = edges.shape[1]
    lanes = pl.ds(lane * 128, 128)
    acc = {}
    for shifted in (0, 1):
        for i in range(edge // 8):
            column = ((-edge, 4 - edge), (cols, cols - 4))[side][shifted] + 8 * i
            x = None
            for j in range(cols // 8):
                t = (column - 8 * j) // 4 + taps // 2
                if 0 <= t < taps:
                    if x is None:
                        x = edges[shifted, pl.ds(8 * i, 8), lanes]
                    term = kb[t, :, lanes] * x
                    acc[j] = acc[j] + term if j in acc else term
    return acc


def stage_edges(edges, halo, side):
    edge = edges.shape[1]
    halo = halo.astype(F32)
    edges[0] = halo
    if side == 0:
        edges[1, pl.ds(0, edge - 4), :] = halo[4:]
    else:
        edges[1, pl.ds(4, edge - 4), :] = halo[: edge - 4]


def inner_kernel(
    core_ref, fields_ref, near_ref, kernel_ref, up_hbm, down_hbm, out_ref, upt_ref, downt_ref,
    s0, s4, kb, edges, up_ref, down_ref, sems,
):
    rows, cols, channels = fields_ref.shape
    taps = kernel_ref.shape[0]
    copies = [
        pltpu.make_async_copy(up_hbm, up_ref, sems.at[0]),
        pltpu.make_async_copy(down_hbm, down_ref, sems.at[1]),
    ]
    for copy in copies:
        copy.start()
    spread_taps(kb, kernel_ref, False)
    s4[...] = jnp.zeros_like(s4)
    edges[...] = jnp.zeros_like(edges)

    def one_row(side, r, carry):
        middle = fields_ref[r].astype(F32)
        s0[...] = middle
        s4[pl.ds(4, cols), :] = middle
        stage_edges(edges, near_ref[r], side)
        for lane in lane_groups(channels):
            lanes = pl.ds(lane * 128, 128)
            weights = [kb[t, :, lanes] for t in range(taps)]
            acc = [None] * (cols // 8)
            for i in range(cols // 8 + 1):
                for half, ref in ((0, s0), (1, s4)):
                    if half == 0 and i == cols // 8:
                        continue
                    x = ref[pl.ds(8 * i, 8), lanes]
                    for j in range(cols // 8):
                        t = 2 * (i - j) - half + taps // 2
                        if 0 <= t < taps:
                            add_to(acc, j, weights[t] * x)
            for j, value in halo_terms(edges, kb, lane, cols, taps, side).items():
                add_to(acc, j, value)
            for j, value in enumerate(acc):
                out_ref[r, pl.ds(8 * j, 8), lanes] = value
        return carry

    for side, here in ((1, core_ref[0] == 0), (0, core_ref[0] != 0)):

        @pl.when(here)
        def _(side=side):
            lax.fori_loop(0, rows, functools.partial(one_row, side), 0)

    for copy in copies:
        copy.wait()
    for j in range(up_ref.shape[1] // 256):
        part = pl.ds(256 * j, 256)
        upt_ref[part, :] = up_ref[:, part].T
        downt_ref[:, part] = down_ref[part, :].T


def inner(core, fields, near, kernel, up, down):
    rows, cols, channels = fields.shape
    taps, edge = kernel.shape[0], near.shape[1]
    return pl.pallas_call(
        inner_kernel,
        in_specs=[pl.BlockSpec(memory_space=pltpu.SMEM)]
        + [resident()] * 3
        + [pl.BlockSpec(memory_space=pltpu.HBM)] * 2,
        out_specs=[resident()] * 3,
        out_shape=[resident_shape(rows, cols, channels), pltpu.VMEM(down.shape, BF16), pltpu.VMEM(up.shape, BF16)],
        scratch_shapes=[
            pltpu.VMEM((cols, channels), F32),
            pltpu.VMEM((cols + 8, channels), F32),
            pltpu.VMEM((taps, 8, channels), F32),
            pltpu.VMEM((2, edge, channels), F32),
            pltpu.VMEM(up.shape, BF16),
            pltpu.VMEM(down.shape, BF16),
            pltpu.SemaphoreType.DMA((2,)),
        ],
        compiler_params=pltpu.CompilerParams(vmem_limit_bytes=8 * 2**20),
        cost_estimate=pl.CostEstimate(
            flops=260 * taps * rows * cols * channels, transcendentals=0,
            bytes_accessed=rows * cols * channels * 6,
        ),
        name="inner",
    )(core, fields, near, kernel, up, down)


def forward_kernel(
    reach, first, last, start, core_ref, inner_ref, far_ref, fields_ref, cot_ref, kernel_ref,
    up_ref, upt_ref, down_ref, downt_ref, *refs,
):
    given, refs = ((), refs) if first else (refs[2:4], refs[4:])
    (out_ref, grad_ref, gup_ref, gdt_ref), refs = refs[:4], refs[4:]
    if reach:
        (near_out_ref, far_out_ref), refs = refs[:2], refs[2:]
        edges, kb, conv_s = refs[:3]
        refs = refs[3:]
    normed_s, act_s, hg_s = refs[:3]
    gup_s, gdt_s = refs[3:] if last else (gup_ref, gdt_ref)
    step = pl.program_id(0)
    _, cols, channels = inner_ref.shape
    edge, taps = far_ref.shape[1], kernel_ref.shape[0]
    rows = far_ref.shape[0] if reach else NEAR_BLOCK
    base_row = start + step * rows
    here = pl.ds(base_row, rows)
    even = core_ref[0] == 0
    hid = up_ref.shape[1]
    width = 256
    count = edge if reach else cols - edge
    cells = rows * count
    if reach:
        place = jnp.where(even, 0, cols - edge)
    else:
        place = jnp.where(even, edge, 0)
    span = pl.ds(pl.multiple_of(place, 16), count)

    @pl.when(step == 0)
    def _():
        if first:
            gup_s[...] = jnp.zeros_like(gup_s)
            gdt_s[...] = jnp.zeros_like(gdt_s)
        if last:
            gup_s[...] = given[0][...]
            gdt_s[...] = given[1][...]
        if reach:
            spread_taps(kb, kernel_ref, False)
            edges[...] = jnp.zeros_like(edges)

    if reach:

        def one_row(side, r, carry):
            stage_edges(edges, far_ref[r], side)
            for lane in lane_groups(channels):
                lanes = pl.ds(lane * 128, 128)
                terms = halo_terms(edges, kb, lane, cols, taps, side)
                skip = (cols - edge) // 8 if side else 0
                for j in range(count // 8):
                    base = inner_ref[base_row + r, pl.ds(8 * (j + skip), 8), lanes]
                    conv_s[r, pl.ds(8 * j, 8), lanes] = base + terms[j + skip] if j + skip in terms else base
            return carry

        for side, mine in ((0, even), (1, jnp.logical_not(even))):

            @pl.when(mine)
            def _(side=side):
                lax.fori_loop(0, rows, functools.partial(one_row, side), 0)

        conv = conv_s[...].reshape(cells, channels)
    else:
        conv = inner_ref[here, span, :].reshape(cells, channels)
    center = jnp.mean(conv, axis=-1, keepdims=True)
    deviation = conv - center
    spread = jnp.mean(deviation * deviation, axis=-1, keepdims=True)
    inv_scale = lax.rsqrt(spread + 1e-06)
    normed = deviation * inv_scale
    normed_s[...] = normed
    low = normed.astype(BF16)
    cot = cot_ref[here, span, :].reshape(cells, channels)
    over_cells = (((0,), (0,)), ((), ()))
    for j in range(hid // width):
        part = pl.ds(j * width, width)
        h = jnp.dot(low, up_ref[:, part], preferred_element_type=F32)
        u = jnp.dot(cot, downt_ref[:, part], preferred_element_type=F32)
        inner = h * (GELU_A + GELU_B * (h * h))
        t = jnp.tanh(inner)
        rise = 1.0 + t
        act_s[:, part] = (0.5 * h * rise).astype(BF16)
        slope = rise * (0.5 + (1.0 - t) * (1.5 * inner - GELU_A * h))
        hg_s[:, part] = (u * slope).astype(BF16)
    out = jnp.dot(act_s[...], down_ref[...], preferred_element_type=F32)
    out = out + fields_ref[here, span, :].reshape(cells, channels).astype(F32)
    normed_grad = jnp.dot(hg_s[...], upt_ref[...], preferred_element_type=F32)
    for j in range(hid // width):
        part = pl.ds(j * width, width)
        gup_s[j] += lax.dot_general(low, hg_s[:, part], over_cells, preferred_element_type=F32)
        gdt_s[:, part] += lax.dot_general(cot, act_s[:, part], over_cells, preferred_element_type=F32)
    out_ref[here, span, :] = out.astype(BF16).reshape(rows, count, channels)
    normed = normed_s[...]
    mean_grad = jnp.mean(normed_grad, axis=-1, keepdims=True)
    mean_cross = jnp.mean(normed_grad * normed, axis=-1, keepdims=True)
    grad = inv_scale * (normed_grad - mean_grad - normed * mean_cross)
    grad = grad.reshape(rows, count, channels)
    grad_ref[here, span, :] = grad
    if reach:
        far_out_ref[...] = grad.astype(BF16)
        near_place = jnp.where(even, cols - edge, 0)
        near_out_ref[...] = grad_ref[here, pl.ds(pl.multiple_of(near_place, 16), edge), :].astype(BF16)

    if last:
        mine_ref, theirs_ref = gup_ref, gdt_ref
        ending = step == pl.num_programs(0) - 1

        @pl.when(ending & even)
        def _():
            for j in range(hid // width):
                part = pl.ds(j * width, width)
                mine_ref[part, :] = gup_s[j]
                theirs_ref[part, :] = gdt_s[:, part].T.astype(BF16)

        @pl.when(ending & jnp.logical_not(even))
        def _():
            for j in range(hid // width):
                part = pl.ds(j * width, width)
                theirs_ref[part, :] = gup_s[j].astype(BF16)
                mine_ref[part, :] = gdt_s[:, part].T


def forward(core, conv_inner, far, fields, cot, kernel, up, up_t, down, down_t, carried, reach, begin, end):
    rows, cols, channels = cot.shape
    edge = far.shape[1]
    taps, hid = kernel.shape[0], up.shape[1]
    count = edge if reach else cols - edge
    cells = (end - begin) * count
    last = reach and end == rows
    block = end - begin if reach else NEAR_BLOCK
    own = row_spec(block, edge, channels)
    sums = [(hid // 256, channels, 256), (channels, hid)]
    ends = [((hid, channels), F32), ((hid, channels), BF16)] if last else [(s, F32) for s in sums]
    edges_out = [jax.ShapeDtypeStruct((end - begin, edge, channels), BF16)] * (2 if reach else 0)
    block_cells = block * count
    return pl.pallas_call(
        functools.partial(forward_kernel, reach, not carried, last, begin),
        grid=((end - begin) // block,),
        in_specs=[pl.BlockSpec(memory_space=pltpu.SMEM), resident(), own if reach else resident()]
        + [resident()] * (7 + len(carried)),
        out_specs=[resident()] * 4 + [own] * len(edges_out),
        out_shape=[pltpu.VMEM((rows, cols, channels), BF16), resident_shape(rows, cols, channels)]
        + [pltpu.VMEM(s, d) for s, d in ends]
        + edges_out,
        input_output_aliases={} if not carried else {10: 0, 11: 1} if last else {10: 0, 11: 1, 12: 2, 13: 3},
        scratch_shapes=(
            [
                pltpu.VMEM((2, edge, channels), F32),
                pltpu.VMEM((taps, 8, channels), F32),
                pltpu.VMEM((block, count, channels), F32),
            ]
            if reach
            else []
        )
        + [
            pltpu.VMEM((block_cells, channels), F32),
            pltpu.VMEM((block_cells, hid), BF16),
            pltpu.VMEM((block_cells, hid), BF16),
        ]
        + ([pltpu.VMEM(s, F32) for s in sums] if last else []),
        compiler_params=params(28),
        cost_estimate=pl.CostEstimate(
            flops=28 * cells * channels * hid, transcendentals=cells * hid,
            bytes_accessed=cells * channels * 12,
        ),
        name="forward",
    )(core, conv_inner, far, fields, cot, kernel, up, up_t, down, down_t, *carried)


def kernel_grad_kernel(start, core_ref, fields_ref, near_ref, far_ref, grad_ref, given_ref, out_ref, s0, s4, sums):
    _, cols, channels = fields_ref.shape
    rows, edge, _ = far_ref.shape
    even = core_ref[0] == 0
    taps = out_ref.shape[0] - 1
    blocks = cols // 8

    sums[...] = jnp.zeros_like(sums)

    def one_row(r, carry):
        left, right = halo_row(even, near_ref[start + r], far_ref[r])
        stage_row(s0, s4, left, fields_ref[start + r], right)
        for lane in lane_groups(channels):
            lanes = pl.ds(lane * 128, 128)
            grads = [grad_ref[start + r, pl.ds(8 * j, 8), lanes] for j in range(blocks)]
            acc = [None] * taps
            for i, half, uses in tap_uses(blocks, taps, edge):
                x = (s4 if half else s0)[pl.ds(8 * i, 8), lanes]
                for j, t in uses:
                    add_to(acc, t, grads[j] * x)
            for t in range(taps):
                sums[t, :, lanes] += acc[t]
        return carry

    lax.fori_loop(0, rows, one_row, 0)

    for t in range(taps):
        here = jnp.sum(sums[t], axis=0, keepdims=True)
        out_ref[pl.ds(t, 1), :] = given_ref[pl.ds(t, 1), :] + here
    out_ref[pl.ds(taps, 1), :] = jnp.zeros((1, channels), F32)


def staging(cols, edge, channels):
    return [
        pltpu.VMEM((cols + 2 * edge, channels), F32),
        pltpu.VMEM((cols + 2 * edge - 8, channels), F32),
    ]


def kernel_grad(core, fields, near, far, grad, given, start):
    _, cols, channels = fields.shape
    count, edge, _ = far.shape
    taps = given.shape[0] - 1
    return pl.pallas_call(
        functools.partial(kernel_grad_kernel, start),
        in_specs=[pl.BlockSpec(memory_space=pltpu.SMEM)] + [resident()] * 5,
        out_specs=resident(),
        out_shape=resident_shape(taps + 1, channels),
        scratch_shapes=staging(cols, edge, channels) + [pltpu.VMEM((taps, 8, channels), F32)],
        compiler_params=pltpu.CompilerParams(vmem_limit_bytes=8 * 2**20),
        cost_estimate=pl.CostEstimate(
            flops=60 * taps * count * cols * channels, transcendentals=0,
            bytes_accessed=count * cols * channels * 8,
        ),
        name="kernel_grad",
    )(core, fields, near, far, grad, given)


def backward_kernel(start, core_ref, grad_ref, near_ref, far_ref, cot_ref, kernel_ref, *refs):
    out_ref, s0, s4, kb = refs[-4:]
    _, cols, channels = grad_ref.shape
    rows, edge, _ = far_ref.shape
    even = core_ref[0] == 0
    base = start + pl.program_id(0) * rows
    taps = kernel_ref.shape[0]

    @pl.when(pl.program_id(0) == 0)
    def _():
        spread_taps(kb, kernel_ref, True)

    def one_row(r, carry):
        left, right = halo_row(even, near_ref[base + r], far_ref[r])
        stage_row(s0, s4, left, grad_ref[base + r], right)
        for lane in lane_groups(channels):
            acc = conv_lane(s0, s4, kb, lane, cols, taps, edge)
            lanes = pl.ds(lane * 128, 128)
            back = jnp.concatenate(acc, axis=0) + cot_ref[r, :, lanes].astype(F32)
            out_ref[r, :, lanes] = back.astype(BF16)
        return carry

    lax.fori_loop(0, rows, one_row, 0)


def backward(core, grad, near, far, cot, kernel, carried, start):
    rows, cols, channels = grad.shape
    count, edge, _ = far.shape
    taps = kernel.shape[0]
    own = functools.partial(row_spec, BLOCK)
    at = pl.BlockSpec((BLOCK, cols, channels), lambda i: (i + start // BLOCK, 0, 0))
    return pl.pallas_call(
        functools.partial(backward_kernel, start),
        grid=(count // BLOCK,),
        in_specs=[
            pl.BlockSpec(memory_space=pltpu.SMEM), resident(), resident(), own(edge, channels), at, resident(),
        ]
        + [pl.BlockSpec(memory_space=pl.ANY)] * len(carried),
        out_specs=at,
        out_shape=jax.ShapeDtypeStruct((rows, cols, channels), BF16),
        input_output_aliases={6: 0} if carried else {},
        scratch_shapes=staging(cols, edge, channels) + [pltpu.VMEM((taps, 8, channels), F32)],
        compiler_params=params(8),
        cost_estimate=pl.CostEstimate(
            flops=60 * taps * count * cols * channels, transcendentals=0,
            bytes_accessed=count * cols * channels * 10,
        ),
        name="backward",
    )(core, grad, near, far, cot, kernel, *carried)


def finish_kernel(factor, core_ref, own_ref, got_ref, tail_ref, kgrad_ref, up_ref, down_ref, taps_ref):
    even = core_ref[0] == 0
    width = own_ref.shape[1]
    for j in range(own_ref.shape[0] // width):
        part = pl.ds(j * width, width)
        own, got = own_ref[part, :].astype(F32) * factor, got_ref[part, :].astype(F32) * factor
        up_ref[:, part] = jnp.where(even, own, got)
        down_ref[part, :] = jnp.where(even, got, own)
    taps = taps_ref.shape[0]
    taps_ref[...] = (kgrad_ref[pl.ds(0, taps), :] + tail_ref[pl.ds(0, taps), :].astype(F32)) * factor


def finish(core, own, got, kgrad, taps, factor):
    hid, channels = own.shape[0] - kgrad.shape[0], own.shape[1]
    rows = hid // 2
    part = pl.BlockSpec((rows, channels), lambda j: (j, 0))
    return pl.pallas_call(
        functools.partial(finish_kernel, factor),
        grid=(hid // rows,),
        in_specs=[
            pl.BlockSpec(memory_space=pltpu.SMEM), part, part,
            pl.BlockSpec(kgrad.shape, lambda j: (hid // kgrad.shape[0], 0)), whole_spec(*kgrad.shape),
        ],
        out_specs=[
            pl.BlockSpec((channels, rows), lambda j: (0, j)), part, whole_spec(taps, channels),
        ],
        out_shape=[
            jax.ShapeDtypeStruct((channels, hid), F32),
            jax.ShapeDtypeStruct((hid, channels), F32),
            jax.ShapeDtypeStruct((taps, channels), F32),
        ],
        compiler_params=params(8),
        name="finish",
    )(core, own, got, got, kgrad)


def after(values, *others):
    held, _ = lax.optimization_barrier((values, others))
    return held


def chunk_starts(rows):
    first = rows // 2 // BLOCK * BLOCK
    return [0, first, rows]


def with_places(fields):
    found = groups()
    core = found[0][0][0]
    fields, places, index, even = lax.optimization_barrier(
        (fields, [places for places, _ in found], core.astype(jnp.int32).reshape(1), core == 0)
    )
    return fields, [(p, masks) for p, (_, masks) in zip(places, found)], index, even


def per_device(fields, cotangent, kernel, up_weight, down_weight):
    rows, cols, channels = fields.shape
    taps, hid = kernel.shape[0], up_weight.shape[1]
    edge = -(-KERNEL_SPACING * (taps // 2) // 8) * 8
    fields, (core, plane, depth), index, even = with_places(fields)
    bounds = chunk_starts(rows)
    chunks = list(zip(bounds[:-1], bounds[1:]))
    to_left, to_right = fields[:, :edge], fields[:, cols - edge :]
    near_out, far_out = jnp.where(even, to_right, to_left), jnp.where(even, to_left, to_right)
    middle = chunks[0][1]
    near = on_chip(near_out)
    far = [off_chip(far_out[:middle])]
    near, _ = lax.optimization_barrier((near, far_out))
    conv_inner, up_t, down_t = inner(index, fields, near, kernel, up_weight, down_weight)
    far_out = after(far_out, conv_inner)
    far.append(off_chip(far_out[middle:]))

    def cells_of(carried, reach, halo, begin, end):
        return forward(
            index, conv_inner, halo, fields, cotangent, kernel, up_weight, up_t, down_weight, down_t,
            carried, reach, begin, end,
        )

    carried = cells_of((), False, near, 0, rows)
    grad_near, grad_far = [], []
    for (begin, end), arrived in zip(chunks, far):
        *carried, near_edge, far_edge = cells_of(carried, True, arrived, begin, end)
        grad_near.append(near_edge)
        if end < rows:
            grad_far.append(off_chip(far_edge))
    output, grad, mine, theirs = carried

    kgrad = jnp.zeros((taps + 1, channels), F32)

    def add_kernel_grad(total, which):
        return kernel_grad(index, fields, near, far[which], grad, total, chunks[which][0])

    def add_field_grad(so_far, which):
        return (
            backward(index, grad, grad_near, grad_far[which], cotangent, kernel, so_far, chunks[which][0]),
        )

    quarter = hid // 4
    got = [xor_permute(theirs[i : i + quarter], core[1][1]) for i in range(0, hid, quarter)]
    part = mine + jnp.concatenate(got, axis=0).astype(F32)
    sends, total = scatter_stage(part, plane)
    sends = after(sends, grad_far[0])
    kgrad = after(kgrad, *sends)
    kgrad = add_kernel_grad(kgrad, 0)
    part, kgrad = scatter_finish(sends, total, plane, kgrad)
    part, far_edge = lax.optimization_barrier((part, far_edge))
    grad_far.append(off_chip(far_edge))
    grad_near = on_chip(jnp.concatenate(grad_near, axis=0))
    sends, total = scatter_stage(part, depth)
    sends, kgrad = lax.optimization_barrier((sends, kgrad))
    kgrad = add_kernel_grad(kgrad, 1)
    part, kgrad = scatter_finish(sends, total, depth, kgrad)
    part = part.astype(BF16)
    packed = pack(part, kgrad)
    grad_far, _ = lax.optimization_barrier((grad_far, packed))
    field_grad = add_field_grad((), 0)
    part, kgrad, field_grad = gather_finish(packed, kgrad, depth, field_grad)
    packed = pack(part, kgrad)
    field_grad, grad_far[1] = lax.optimization_barrier((field_grad, after(grad_far[1], packed)))
    field_grad = add_field_grad(field_grad, 1)
    part, kgrad, field_grad = gather_finish(packed, kgrad, plane, field_grad)
    packed = pack(part, kgrad)
    got = on_chip(packed)
    factor = 1.0 / math.sqrt(rows * cols * lax.axis_size("lon") * lax.axis_size("lat"))
    up_grad, down_grad, tap_grad = finish(index, packed, got, kgrad, taps, factor)
    return (output, field_grad[0], tap_grad, up_grad, down_grad)


def solution(mesh):
    placed = (P("lat", "lon", None), P("lat", "lon", None), P(), P(), P())
    return jax.shard_map(
        per_device,
        mesh=mesh,
        in_specs=placed,
        out_specs=(P("lat", "lon", None), P("lat", "lon", None), P(), P(), P()),
        check_vma=False,
    )
```

```python
import functools
import math

import jax
import jax.numpy as jnp
from jax import lax
from jax.experimental import pallas as pl
from jax.experimental.pallas import tpu as pltpu
from jax.sharding import PartitionSpec as P

KERNEL_SPACING = 4
BLOCK = 4
NEAR_BLOCK = 32
FAR_BLOCK = 16
AXES = ("lon", "lat")
F32 = jnp.float32
BF16 = jnp.bfloat16
GELU_A = math.sqrt(2.0 / math.pi)
GELU_B = GELU_A * 0.044715


def xor_permute(value, mask):
    nlon, nlat = lax.axis_size("lon"), lax.axis_size("lat")
    lat_mask, lon_mask = mask
    pairs = [
        (lon * nlat + lat, (lon ^ lon_mask) * nlat + (lat ^ lat_mask))
        for lon in range(nlon)
        for lat in range(nlat)
    ]
    return lax.ppermute(value, AXES, pairs)


def on_chip(value):
    return xor_permute(value, (0, 1))


def off_chip(value):
    count = lax.axis_size("lon")
    pairs = [(i, (i + (1 if i % 2 else -1)) % count) for i in range(count)]
    return lax.ppermute(value, "lon", pairs)


def groups():
    nlon, nlat = lax.axis_size("lon"), lax.axis_size("lat")
    lon, lat = lax.axis_index("lon").astype(jnp.uint32), lax.axis_index("lat").astype(jnp.uint32)
    core = (lon & 1, [(0, s) for s in range(2)])
    plane = (lat * 2 + ((lon >> 1) & 1), [(s >> 1, (s & 1) * 2) for s in range(2 * nlat)])
    depth = (lon >> 2, [(0, s * 4) for s in range(nlon // 4)])
    return [([own ^ jnp.uint32(s) for s in range(len(masks))], masks) for own, masks in (core, plane, depth)]


def piece(parts, place):
    zero = jnp.uint32(0)
    return lax.dynamic_slice(parts, (place, zero, zero), (1,) + parts.shape[1:])[0]


def scatter_stage(value, group):
    places, _ = group
    size = len(places)
    parts = value.reshape(size, value.shape[0] // size, value.shape[1])
    return [piece(parts, p).astype(BF16) for p in places[1:]], piece(parts, places[0])


def scatter_finish(sends, total, group, beside):
    _, masks = group
    got, beside = lax.optimization_barrier(([xor_permute(v, m) for v, m in zip(sends, masks[1:])], beside))
    for part in got:
        total = total + part.astype(F32)
    return total, beside


def gather_finish(packed, extra, group, beside):
    places, masks = group
    size = len(places)
    rows = packed.shape[0] - extra.shape[0]
    got = [packed[:rows]]
    parts, beside = lax.optimization_barrier(([xor_permute(packed, m) for m in masks[1:]], beside))
    for part in parts:
        got.append(part[:rows])
        extra = extra + part[rows:].astype(F32)
    whole = jnp.zeros((size, rows, packed.shape[1]), packed.dtype)
    zero = jnp.uint32(0)
    for part, place in zip(got, places):
        whole = lax.dynamic_update_slice(whole, part[None], (place, zero, zero))
    return whole.reshape(size * rows, packed.shape[1]), extra, beside


def pack(value, extra):
    return jnp.concatenate([value, extra.astype(BF16)], axis=0)


def lane_groups(channels):
    return range(channels // 128)


def halo_row(even, near, far):
    return jnp.where(even, far, near), jnp.where(even, near, far)


def stage_row(s0, s4, left, middle, right):
    edge, cols = left.shape[0], middle.shape[0]
    left, middle, right = left.astype(F32), middle.astype(F32), right.astype(F32)
    s0[pl.ds(0, edge), :] = left
    s0[pl.ds(edge, cols), :] = middle
    s0[pl.ds(edge + cols, edge), :] = right
    s4[pl.ds(0, edge - 4), :] = left[4:]
    s4[pl.ds(edge - 4, cols), :] = middle
    s4[pl.ds(edge - 4 + cols, edge - 4), :] = right[: edge - 4]


def spread_taps(kb, kernel_ref, flip):
    taps = kernel_ref.shape[0]
    for t in range(taps):
        row = kernel_ref[pl.ds(taps - 1 - t if flip else t, 1), :]
        kb[t] = jnp.broadcast_to(row, kb.shape[1:])


def tap_uses(blocks, taps, edge):
    lead = (edge - KERNEL_SPACING * (taps // 2)) // 4
    result = []
    for i in range(blocks + 2 * edge // 8):
        for half in (0, 1):
            uses = []
            for j in range(blocks):
                t = 2 * (i - j) + half - lead
                if 0 <= t < taps:
                    uses.append((j, t))
            if uses:
                result.append((i, half, uses))
    return result


def add_to(acc, at, term):
    acc[at] = term if acc[at] is None else acc[at] + term


def conv_lane(s0, s4, kb, lane, cols, taps, edge):
    lanes = pl.ds(lane * 128, 128)
    acc = [None] * (cols // 8)
    weights = [kb[t, :, lanes] for t in range(taps)]
    for i, half, uses in tap_uses(cols // 8, taps, edge):
        x = (s4 if half else s0)[pl.ds(8 * i, 8), lanes]
        for j, t in uses:
            add_to(acc, j, weights[t] * x)
    return acc


def row_spec(block, n, width):
    return pl.BlockSpec((block, n, width), lambda i: (i, 0, 0))


def whole_spec(*shape):
    return pl.BlockSpec(shape, lambda i: (0,) * len(shape))


def resident():
    return pl.BlockSpec(memory_space=pltpu.VMEM)


def resident_shape(*shape):
    return pltpu.VMEM(shape, F32)


def params(mib):
    return pltpu.CompilerParams(dimension_semantics=("arbitrary",), vmem_limit_bytes=mib * 2**20)


def halo_terms(edges, kb, lane, cols, taps, side):
    edge = edges.shape[1]
    lanes = pl.ds(lane * 128, 128)
    acc = {}
    for shifted in (0, 1):
        for i in range(edge // 8):
            column = ((-edge, 4 - edge), (cols, cols - 4))[side][shifted] + 8 * i
            x = None
            for j in range(cols // 8):
                t = (column - 8 * j) // 4 + taps // 2
                if 0 <= t < taps:
                    if x is None:
                        x = edges[shifted, pl.ds(8 * i, 8), lanes]
                    term = kb[t, :, lanes] * x
                    acc[j] = acc[j] + term if j in acc else term
    return acc


def stage_edges(edges, halo, side):
    edge = edges.shape[1]
    halo = halo.astype(F32)
    edges[0] = halo
    if side == 0:
        edges[1, pl.ds(0, edge - 4), :] = halo[4:]
    else:
        edges[1, pl.ds(4, edge - 4), :] = halo[: edge - 4]


def inner_kernel(
    core_ref, fields_ref, near_ref, kernel_ref, up_hbm, down_hbm, out_ref, upt_ref, downt_ref,
    s0, s4, kb, edges, up_ref, down_ref, sems,
):
    rows, cols, channels = fields_ref.shape
    taps = kernel_ref.shape[0]
    copies = [
        pltpu.make_async_copy(up_hbm, up_ref, sems.at[0]),
        pltpu.make_async_copy(down_hbm, down_ref, sems.at[1]),
    ]
    for copy in copies:
        copy.start()
    spread_taps(kb, kernel_ref, False)
    s4[...] = jnp.zeros_like(s4)
    edges[...] = jnp.zeros_like(edges)

    def one_row(side, r, carry):
        middle = fields_ref[r].astype(F32)
        s0[...] = middle
        s4[pl.ds(4, cols), :] = middle
        stage_edges(edges, near_ref[r], side)
        for lane in lane_groups(channels):
            lanes = pl.ds(lane * 128, 128)
            weights = [kb[t, :, lanes] for t in range(taps)]
            acc = [None] * (cols // 8)
            for i in range(cols // 8 + 1):
                for half, ref in ((0, s0), (1, s4)):
                    if half == 0 and i == cols // 8:
                        continue
                    x = ref[pl.ds(8 * i, 8), lanes]
                    for j in range(cols // 8):
                        t = 2 * (i - j) - half + taps // 2
                        if 0 <= t < taps:
                            add_to(acc, j, weights[t] * x)
            for j, value in halo_terms(edges, kb, lane, cols, taps, side).items():
                add_to(acc, j, value)
            for j, value in enumerate(acc):
                out_ref[r, pl.ds(8 * j, 8), lanes] = value
        return carry

    for side, here in ((1, core_ref[0] == 0), (0, core_ref[0] != 0)):

        @pl.when(here)
        def _(side=side):
            lax.fori_loop(0, rows, functools.partial(one_row, side), 0)

    for copy in copies:
        copy.wait()


def inner(core, fields, near, kernel, up, down):
    rows, cols, channels = fields.shape
    taps, edge = kernel.shape[0], near.shape[1]
    return pl.pallas_call(
        inner_kernel,
        in_specs=[pl.BlockSpec(memory_space=pltpu.SMEM)]
        + [resident()] * 3
        + [pl.BlockSpec(memory_space=pltpu.HBM)] * 2,
        out_specs=[resident()] * 3,
        out_shape=[resident_shape(rows, cols, channels), pltpu.VMEM(down.shape, BF16), pltpu.VMEM(up.shape, BF16)],
        scratch_shapes=[
            pltpu.VMEM((cols, channels), F32),
            pltpu.VMEM((cols + 8, channels), F32),
            pltpu.VMEM((taps, 8, channels), F32),
            pltpu.VMEM((2, edge, channels), F32),
            pltpu.VMEM(up.shape, BF16),
            pltpu.VMEM(down.shape, BF16),
            pltpu.SemaphoreType.DMA((2,)),
        ],
        compiler_params=pltpu.CompilerParams(vmem_limit_bytes=8 * 2**20),
        cost_estimate=pl.CostEstimate(
            flops=260 * taps * rows * cols * channels, transcendentals=0,
            bytes_accessed=rows * cols * channels * 6,
        ),
        name="inner",
    )(core, fields, near, kernel, up, down)


def forward_kernel(
    reach, first, last, start, core_ref, inner_ref, far_ref, fields_ref, cot_ref, kernel_ref,
    up_ref, upt_ref, down_ref, downt_ref, *refs,
):
    given, refs = ((), refs) if first else (refs[2:4], refs[4:])
    (out_ref, grad_ref, gup_ref, gdt_ref), refs = refs[:4], refs[4:]
    if reach:
        (near_out_ref, far_out_ref), refs = refs[:2], refs[2:]
        edges, kb, conv_s = refs[:3]
        refs = refs[3:]
    normed_s, act_s, hg_s = refs[:3]
    gup_s, gdt_s = refs[3:] if last else (gup_ref, gdt_ref)
    step = pl.program_id(0)
    _, cols, channels = inner_ref.shape
    edge, taps = far_ref.shape[1], kernel_ref.shape[0]
    rows = far_ref.shape[0] if reach else NEAR_BLOCK
    base_row = start + step * rows
    here = pl.ds(base_row, rows)
    even = core_ref[0] == 0
    hid = up_ref.shape[1]
    width = 256
    count = edge if reach else cols - edge
    cells = rows * count
    if reach:
        place = jnp.where(even, 0, cols - edge)
    else:
        place = jnp.where(even, edge, 0)
    span = pl.ds(pl.multiple_of(place, 16), count)

    @pl.when(step == 0)
    def _():
        if first:
            gup_s[...] = jnp.zeros_like(gup_s)
            gdt_s[...] = jnp.zeros_like(gdt_s)
        if last:
            gup_s[...] = given[0][...]
            gdt_s[...] = given[1][...]
        if reach:
            spread_taps(kb, kernel_ref, False)
            edges[...] = jnp.zeros_like(edges)

    if reach:

        def one_row(side, r, carry):
            stage_edges(edges, far_ref[r], side)
            for lane in lane_groups(channels):
                lanes = pl.ds(lane * 128, 128)
                terms = halo_terms(edges, kb, lane, cols, taps, side)
                skip = (cols - edge) // 8 if side else 0
                for j in range(count // 8):
                    base = inner_ref[base_row + r, pl.ds(8 * (j + skip), 8), lanes]
                    conv_s[r, pl.ds(8 * j, 8), lanes] = base + terms[j + skip] if j + skip in terms else base
            return carry

        for side, mine in ((0, even), (1, jnp.logical_not(even))):

            @pl.when(mine)
            def _(side=side):
                lax.fori_loop(0, rows, functools.partial(one_row, side), 0)

        conv = conv_s[...].reshape(cells, channels)
    else:
        conv = inner_ref[here, span, :].reshape(cells, channels)
    center = jnp.mean(conv, axis=-1, keepdims=True)
    deviation = conv - center
    spread = jnp.mean(deviation * deviation, axis=-1, keepdims=True)
    inv_scale = lax.rsqrt(spread + 1e-06)
    normed = deviation * inv_scale
    normed_s[...] = normed
    low = normed.astype(BF16)
    cot = cot_ref[here, span, :].reshape(cells, channels)
    over_cells, over_last = (((0,), (0,)), ((), ())), (((1,), (1,)), ((), ()))
    for j in range(hid // width):
        part = pl.ds(j * width, width)
        h = jnp.dot(low, up_ref[:, part], preferred_element_type=F32)
        u = lax.dot_general(cot, down_ref[part, :], over_last, preferred_element_type=F32)
        inner = h * (GELU_A + GELU_B * (h * h))
        t = jnp.tanh(inner)
        rise = 1.0 + t
        act_s[:, part] = (0.5 * h * rise).astype(BF16)
        slope = rise * (0.5 + (1.0 - t) * (1.5 * inner - GELU_A * h))
        hg_s[:, part] = (u * slope).astype(BF16)
    out = jnp.dot(act_s[...], down_ref[...], preferred_element_type=F32)
    out = out + fields_ref[here, span, :].reshape(cells, channels).astype(F32)
    normed_grad = lax.dot_general(hg_s[...], up_ref[...], over_last, preferred_element_type=F32)
    for j in range(hid // width):
        part = pl.ds(j * width, width)
        gup_s[j] += lax.dot_general(low, hg_s[:, part], over_cells, preferred_element_type=F32)
        gdt_s[:, part] += lax.dot_general(cot, act_s[:, part], over_cells, preferred_element_type=F32)
    out_ref[here, span, :] = out.astype(BF16).reshape(rows, count, channels)
    normed = normed_s[...]
    mean_grad = jnp.mean(normed_grad, axis=-1, keepdims=True)
    mean_cross = jnp.mean(normed_grad * normed, axis=-1, keepdims=True)
    grad = inv_scale * (normed_grad - mean_grad - normed * mean_cross)
    grad = grad.reshape(rows, count, channels)
    grad_ref[here, span, :] = grad
    if reach:
        far_out_ref[...] = grad.astype(BF16)
        near_place = jnp.where(even, cols - edge, 0)
        near_out_ref[...] = grad_ref[here, pl.ds(pl.multiple_of(near_place, 16), edge), :].astype(BF16)

    if last:
        mine_ref, theirs_ref = gup_ref, gdt_ref
        ending = step == pl.num_programs(0) - 1

        @pl.when(ending & even)
        def _():
            for j in range(hid // width):
                part = pl.ds(j * width, width)
                mine_ref[part, :] = gup_s[j]
                theirs_ref[part, :] = gdt_s[:, part].T.astype(BF16)

        @pl.when(ending & jnp.logical_not(even))
        def _():
            for j in range(hid // width):
                part = pl.ds(j * width, width)
                theirs_ref[part, :] = gup_s[j].astype(BF16)
                mine_ref[part, :] = gdt_s[:, part].T


def forward(core, conv_inner, far, fields, cot, kernel, up, up_t, down, down_t, carried, reach, begin, end):
    rows, cols, channels = cot.shape
    edge = far.shape[1]
    taps, hid = kernel.shape[0], up.shape[1]
    count = edge if reach else cols - edge
    cells = (end - begin) * count
    last = reach and end == rows
    block = end - begin if reach else NEAR_BLOCK
    own = row_spec(block, edge, channels)
    sums = [(hid // 256, channels, 256), (channels, hid)]
    ends = [((hid, channels), F32), ((hid, channels), BF16)] if last else [(s, F32) for s in sums]
    edges_out = [jax.ShapeDtypeStruct((end - begin, edge, channels), BF16)] * (2 if reach else 0)
    block_cells = block * count
    return pl.pallas_call(
        functools.partial(forward_kernel, reach, not carried, last, begin),
        grid=((end - begin) // block,),
        in_specs=[pl.BlockSpec(memory_space=pltpu.SMEM), resident(), own if reach else resident()]
        + [resident()] * (7 + len(carried)),
        out_specs=[resident()] * 4 + [own] * len(edges_out),
        out_shape=[pltpu.VMEM((rows, cols, channels), BF16), resident_shape(rows, cols, channels)]
        + [pltpu.VMEM(s, d) for s, d in ends]
        + edges_out,
        input_output_aliases={} if not carried else {10: 0, 11: 1} if last else {10: 0, 11: 1, 12: 2, 13: 3},
        scratch_shapes=(
            [
                pltpu.VMEM((2, edge, channels), F32),
                pltpu.VMEM((taps, 8, channels), F32),
                pltpu.VMEM((block, count, channels), F32),
            ]
            if reach
            else []
        )
        + [
            pltpu.VMEM((block_cells, channels), F32),
            pltpu.VMEM((block_cells, hid), BF16),
            pltpu.VMEM((block_cells, hid), BF16),
        ]
        + ([pltpu.VMEM(s, F32) for s in sums] if last else []),
        compiler_params=params(28),
        cost_estimate=pl.CostEstimate(
            flops=28 * cells * channels * hid, transcendentals=cells * hid,
            bytes_accessed=cells * channels * 12,
        ),
        name="forward",
    )(core, conv_inner, far, fields, cot, kernel, up, up_t, down, down_t, *carried)


def kernel_grad_kernel(start, core_ref, fields_ref, near_ref, far_ref, grad_ref, given_ref, out_ref, s0, s4, sums):
    _, cols, channels = fields_ref.shape
    rows, edge, _ = far_ref.shape
    even = core_ref[0] == 0
    taps = out_ref.shape[0] - 1
    blocks = cols // 8

    sums[...] = jnp.zeros_like(sums)

    def one_row(r, carry):
        left, right = halo_row(even, near_ref[start + r], far_ref[r])
        stage_row(s0, s4, left, fields_ref[start + r], right)
        for lane in lane_groups(channels):
            lanes = pl.ds(lane * 128, 128)
            grads = [grad_ref[start + r, pl.ds(8 * j, 8), lanes] for j in range(blocks)]
            acc = [None] * taps
            for i, half, uses in tap_uses(blocks, taps, edge):
                x = (s4 if half else s0)[pl.ds(8 * i, 8), lanes]
                for j, t in uses:
                    add_to(acc, t, grads[j] * x)
            for t in range(taps):
                sums[t, :, lanes] += acc[t]
        return carry

    lax.fori_loop(0, rows, one_row, 0)

    for t in range(taps):
        here = jnp.sum(sums[t], axis=0, keepdims=True)
        out_ref[pl.ds(t, 1), :] = given_ref[pl.ds(t, 1), :] + here
    out_ref[pl.ds(taps, 1), :] = jnp.zeros((1, channels), F32)


def staging(cols, edge, channels):
    return [
        pltpu.VMEM((cols + 2 * edge, channels), F32),
        pltpu.VMEM((cols + 2 * edge - 8, channels), F32),
    ]


def kernel_grad(core, fields, near, far, grad, given, start):
    _, cols, channels = fields.shape
    count, edge, _ = far.shape
    taps = given.shape[0] - 1
    return pl.pallas_call(
        functools.partial(kernel_grad_kernel, start),
        in_specs=[pl.BlockSpec(memory_space=pltpu.SMEM)] + [resident()] * 5,
        out_specs=resident(),
        out_shape=resident_shape(taps + 1, channels),
        scratch_shapes=staging(cols, edge, channels) + [pltpu.VMEM((taps, 8, channels), F32)],
        compiler_params=pltpu.CompilerParams(vmem_limit_bytes=8 * 2**20),
        cost_estimate=pl.CostEstimate(
            flops=60 * taps * count * cols * channels, transcendentals=0,
            bytes_accessed=count * cols * channels * 8,
        ),
        name="kernel_grad",
    )(core, fields, near, far, grad, given)


def backward_kernel(start, core_ref, grad_ref, near_ref, far_ref, cot_ref, kernel_ref, *refs):
    out_ref, s0, s4, kb = refs[-4:]
    _, cols, channels = grad_ref.shape
    rows, edge, _ = far_ref.shape
    even = core_ref[0] == 0
    base = start + pl.program_id(0) * rows
    taps = kernel_ref.shape[0]

    @pl.when(pl.program_id(0) == 0)
    def _():
        spread_taps(kb, kernel_ref, True)

    def one_row(r, carry):
        left, right = halo_row(even, near_ref[base + r], far_ref[r])
        stage_row(s0, s4, left, grad_ref[base + r], right)
        for lane in lane_groups(channels):
            acc = conv_lane(s0, s4, kb, lane, cols, taps, edge)
            lanes = pl.ds(lane * 128, 128)
            back = jnp.concatenate(acc, axis=0) + cot_ref[r, :, lanes].astype(F32)
            out_ref[r, :, lanes] = back.astype(BF16)
        return carry

    lax.fori_loop(0, rows, one_row, 0)


def backward(core, grad, near, far, cot, kernel, carried, start):
    rows, cols, channels = grad.shape
    count, edge, _ = far.shape
    taps = kernel.shape[0]
    own = functools.partial(row_spec, BLOCK)
    at = pl.BlockSpec((BLOCK, cols, channels), lambda i: (i + start // BLOCK, 0, 0))
    return pl.pallas_call(
        functools.partial(backward_kernel, start),
        grid=(count // BLOCK,),
        in_specs=[
            pl.BlockSpec(memory_space=pltpu.SMEM), resident(), resident(), own(edge, channels), at, resident(),
        ]
        + [pl.BlockSpec(memory_space=pl.ANY)] * len(carried),
        out_specs=at,
        out_shape=jax.ShapeDtypeStruct((rows, cols, channels), BF16),
        input_output_aliases={6: 0} if carried else {},
        scratch_shapes=staging(cols, edge, channels) + [pltpu.VMEM((taps, 8, channels), F32)],
        compiler_params=params(8),
        cost_estimate=pl.CostEstimate(
            flops=60 * taps * count * cols * channels, transcendentals=0,
            bytes_accessed=count * cols * channels * 10,
        ),
        name="backward",
    )(core, grad, near, far, cot, kernel, *carried)


def finish_kernel(factor, core_ref, own_ref, got_ref, tail_ref, kgrad_ref, up_ref, down_ref, taps_ref):
    even = core_ref[0] == 0
    width = own_ref.shape[1]
    for j in range(own_ref.shape[0] // width):
        part = pl.ds(j * width, width)
        own, got = own_ref[part, :].astype(F32) * factor, got_ref[part, :].astype(F32) * factor
        up_ref[:, part] = jnp.where(even, own, got)
        down_ref[part, :] = jnp.where(even, got, own)
    taps = taps_ref.shape[0]
    taps_ref[...] = (kgrad_ref[pl.ds(0, taps), :] + tail_ref[pl.ds(0, taps), :].astype(F32)) * factor


def finish(core, own, got, kgrad, taps, factor):
    hid, channels = own.shape[0] - kgrad.shape[0], own.shape[1]
    rows = hid // 2
    part = pl.BlockSpec((rows, channels), lambda j: (j, 0))
    return pl.pallas_call(
        functools.partial(finish_kernel, factor),
        grid=(hid // rows,),
        in_specs=[
            pl.BlockSpec(memory_space=pltpu.SMEM), part, part,
            pl.BlockSpec(kgrad.shape, lambda j: (hid // kgrad.shape[0], 0)), whole_spec(*kgrad.shape),
        ],
        out_specs=[
            pl.BlockSpec((channels, rows), lambda j: (0, j)), part, whole_spec(taps, channels),
        ],
        out_shape=[
            jax.ShapeDtypeStruct((channels, hid), F32),
            jax.ShapeDtypeStruct((hid, channels), F32),
            jax.ShapeDtypeStruct((taps, channels), F32),
        ],
        compiler_params=params(8),
        name="finish",
    )(core, own, got, got, kgrad)


def after(values, *others):
    held, _ = lax.optimization_barrier((values, others))
    return held


def chunk_starts(rows):
    first = rows // 2 // BLOCK * BLOCK
    return [0, first, rows]


def with_places(fields):
    found = groups()
    core = found[0][0][0]
    fields, places, index, even = lax.optimization_barrier(
        (fields, [places for places, _ in found], core.astype(jnp.int32).reshape(1), core == 0)
    )
    return fields, [(p, masks) for p, (_, masks) in zip(places, found)], index, even


def per_device(fields, cotangent, kernel, up_weight, down_weight):
    rows, cols, channels = fields.shape
    taps, hid = kernel.shape[0], up_weight.shape[1]
    edge = -(-KERNEL_SPACING * (taps // 2) // 8) * 8
    fields, (core, plane, depth), index, even = with_places(fields)
    bounds = chunk_starts(rows)
    chunks = list(zip(bounds[:-1], bounds[1:]))
    to_left, to_right = fields[:, :edge], fields[:, cols - edge :]
    near_out, far_out = jnp.where(even, to_right, to_left), jnp.where(even, to_left, to_right)
    middle = chunks[0][1]
    near = on_chip(near_out)
    far = [off_chip(far_out[:middle])]
    near, _ = lax.optimization_barrier((near, far_out))
    conv_inner, up_t, down_t = inner(index, fields, near, kernel, up_weight, down_weight)
    far_out = after(far_out, conv_inner)
    far.append(off_chip(far_out[middle:]))

    def cells_of(carried, reach, halo, begin, end):
        return forward(
            index, conv_inner, halo, fields, cotangent, kernel, up_weight, up_t, down_weight, down_t,
            carried, reach, begin, end,
        )

    carried = cells_of((), False, near, 0, rows)
    grad_near, grad_far = [], []
    for (begin, end), arrived in zip(chunks, far):
        *carried, near_edge, far_edge = cells_of(carried, True, arrived, begin, end)
        grad_near.append(near_edge)
        if end < rows:
            grad_far.append(off_chip(far_edge))
    output, grad, mine, theirs = carried

    kgrad = jnp.zeros((taps + 1, channels), F32)

    def add_kernel_grad(total, which):
        return kernel_grad(index, fields, near, far[which], grad, total, chunks[which][0])

    def add_field_grad(so_far, which):
        return (
            backward(index, grad, grad_near, grad_far[which], cotangent, kernel, so_far, chunks[which][0]),
        )

    quarter = hid // 4
    got = [xor_permute(theirs[i : i + quarter], core[1][1]) for i in range(0, hid, quarter)]
    part = mine + jnp.concatenate(got, axis=0).astype(F32)
    sends, total = scatter_stage(part, plane)
    kgrad = after(kgrad, *sends)
    kgrad = add_kernel_grad(kgrad, 0)
    part, kgrad = scatter_finish(sends, total, plane, kgrad)
    part, far_edge = lax.optimization_barrier((part, far_edge))
    grad_far.append(off_chip(far_edge))
    grad_near = on_chip(jnp.concatenate(grad_near, axis=0))
    sends, total = scatter_stage(part, depth)
    sends = after(sends, grad_far[0])
    sends, kgrad = lax.optimization_barrier((sends, kgrad))
    kgrad = add_kernel_grad(kgrad, 1)
    part, kgrad = scatter_finish(sends, total, depth, kgrad)
    part = part.astype(BF16)
    packed = pack(part, kgrad)
    grad_far, _ = lax.optimization_barrier((grad_far, packed))
    field_grad = add_field_grad((), 0)
    part, kgrad, field_grad = gather_finish(packed, kgrad, depth, field_grad)
    packed = pack(part, kgrad)
    field_grad, grad_far[1] = lax.optimization_barrier((field_grad, after(grad_far[1], packed)))
    field_grad = add_field_grad(field_grad, 1)
    part, kgrad, field_grad = gather_finish(packed, kgrad, plane, field_grad)
    packed = pack(part, kgrad)
    got = on_chip(packed)
    factor = 1.0 / math.sqrt(rows * cols * lax.axis_size("lon") * lax.axis_size("lat"))
    up_grad, down_grad, tap_grad = finish(index, packed, got, kgrad, taps, factor)
    return (output, field_grad[0], tap_grad, up_grad, down_grad)


def solution(mesh):
    placed = (P("lat", "lon", None), P("lat", "lon", None), P(), P(), P())
    return jax.shard_map(
        per_device,
        mesh=mesh,
        in_specs=placed,
        out_specs=(P("lat", "lon", None), P("lat", "lon", None), P(), P(), P()),
        check_vma=False,
    )
```

```python
import functools
import math

import jax
import jax.numpy as jnp
from jax import lax
from jax.experimental import pallas as pl
from jax.experimental.pallas import tpu as pltpu
from jax.sharding import PartitionSpec as P

KERNEL_SPACING = 4
BLOCK = 8
NEAR_BLOCK = 32
FAR_BLOCK = 16
AXES = ("lon", "lat")
F32 = jnp.float32
BF16 = jnp.bfloat16
GELU_A = math.sqrt(2.0 / math.pi)
GELU_B = GELU_A * 0.044715


def xor_permute(value, mask):
    nlon, nlat = lax.axis_size("lon"), lax.axis_size("lat")
    lat_mask, lon_mask = mask
    pairs = [
        (lon * nlat + lat, (lon ^ lon_mask) * nlat + (lat ^ lat_mask))
        for lon in range(nlon)
        for lat in range(nlat)
    ]
    return lax.ppermute(value, AXES, pairs)


def on_chip(value):
    return xor_permute(value, (0, 1))


def off_chip(value):
    count = lax.axis_size("lon")
    pairs = [(i, (i + (1 if i % 2 else -1)) % count) for i in range(count)]
    return lax.ppermute(value, "lon", pairs)


def groups():
    nlon, nlat = lax.axis_size("lon"), lax.axis_size("lat")
    lon, lat = lax.axis_index("lon").astype(jnp.uint32), lax.axis_index("lat").astype(jnp.uint32)
    core = (lon & 1, [(0, s) for s in range(2)])
    plane = (lat * 2 + ((lon >> 1) & 1), [(s >> 1, (s & 1) * 2) for s in range(2 * nlat)])
    depth = (lon >> 2, [(0, s * 4) for s in range(nlon // 4)])
    return [([own ^ jnp.uint32(s) for s in range(len(masks))], masks) for own, masks in (core, plane, depth)]


def piece(parts, place):
    zero = jnp.uint32(0)
    return lax.dynamic_slice(parts, (place, zero, zero), (1,) + parts.shape[1:])[0]


def scatter_stage(value, group):
    places, _ = group
    size = len(places)
    parts = value.reshape(size, value.shape[0] // size, value.shape[1])
    return [piece(parts, p).astype(BF16) for p in places[1:]], piece(parts, places[0])


def scatter_finish(sends, total, group, beside):
    _, masks = group
    got, beside = lax.optimization_barrier(([xor_permute(v, m) for v, m in zip(sends, masks[1:])], beside))
    for part in got:
        total = total + part.astype(F32)
    return total, beside


def gather_finish(packed, extra, group, beside):
    places, masks = group
    size = len(places)
    rows = packed.shape[0] - extra.shape[0]
    got = [packed[:rows]]
    parts, beside = lax.optimization_barrier(([xor_permute(packed, m) for m in masks[1:]], beside))
    for part in parts:
        got.append(part[:rows])
        extra = extra + part[rows:].astype(F32)
    whole = jnp.zeros((size, rows, packed.shape[1]), packed.dtype)
    zero = jnp.uint32(0)
    for part, place in zip(got, places):
        whole = lax.dynamic_update_slice(whole, part[None], (place, zero, zero))
    return whole.reshape(size * rows, packed.shape[1]), extra, beside


def pack(value, extra):
    return jnp.concatenate([value, extra.astype(BF16)], axis=0)


def lane_groups(channels):
    return range(channels // 128)


def halo_row(even, near, far):
    return jnp.where(even, far, near), jnp.where(even, near, far)


def stage_row(s0, s4, left, middle, right):
    edge, cols = left.shape[0], middle.shape[0]
    left, middle, right = left.astype(F32), middle.astype(F32), right.astype(F32)
    s0[pl.ds(0, edge), :] = left
    s0[pl.ds(edge, cols), :] = middle
    s0[pl.ds(edge + cols, edge), :] = right
    s4[pl.ds(0, edge - 4), :] = left[4:]
    s4[pl.ds(edge - 4, cols), :] = middle
    s4[pl.ds(edge - 4 + cols, edge - 4), :] = right[: edge - 4]


def spread_taps(kb, kernel_ref, flip):
    taps = kernel_ref.shape[0]
    for t in range(taps):
        row = kernel_ref[pl.ds(taps - 1 - t if flip else t, 1), :]
        kb[t] = jnp.broadcast_to(row, kb.shape[1:])


def tap_uses(blocks, taps, edge):
    lead = (edge - KERNEL_SPACING * (taps // 2)) // 4
    result = []
    for i in range(blocks + 2 * edge // 8):
        for half in (0, 1):
            uses = []
            for j in range(blocks):
                t = 2 * (i - j) + half - lead
                if 0 <= t < taps:
                    uses.append((j, t))
            if uses:
                result.append((i, half, uses))
    return result


def add_to(acc, at, term):
    acc[at] = term if acc[at] is None else acc[at] + term


def conv_lane(s0, s4, kb, lane, cols, taps, edge):
    lanes = pl.ds(lane * 128, 128)
    acc = [None] * (cols // 8)
    weights = [kb[t, :, lanes] for t in range(taps)]
    for i, half, uses in tap_uses(cols // 8, taps, edge):
        x = (s4 if half else s0)[pl.ds(8 * i, 8), lanes]
        for j, t in uses:
            add_to(acc, j, weights[t] * x)
    return acc


def row_spec(block, n, width):
    return pl.BlockSpec((block, n, width), lambda i: (i, 0, 0))


def whole_spec(*shape):
    return pl.BlockSpec(shape, lambda i: (0,) * len(shape))


def resident():
    return pl.BlockSpec(memory_space=pltpu.VMEM)


def resident_shape(*shape):
    return pltpu.VMEM(shape, F32)


def params(mib):
    return pltpu.CompilerParams(dimension_semantics=("arbitrary",), vmem_limit_bytes=mib * 2**20)


def halo_terms(edges, kb, lane, cols, taps, side):
    edge = edges.shape[1]
    lanes = pl.ds(lane * 128, 128)
    acc = {}
    for shifted in (0, 1):
        for i in range(edge // 8):
            column = ((-edge, 4 - edge), (cols, cols - 4))[side][shifted] + 8 * i
            x = None
            for j in range(cols // 8):
                t = (column - 8 * j) // 4 + taps // 2
                if 0 <= t < taps:
                    if x is None:
                        x = edges[shifted, pl.ds(8 * i, 8), lanes]
                    term = kb[t, :, lanes] * x
                    acc[j] = acc[j] + term if j in acc else term
    return acc


def stage_edges(edges, halo, side):
    edge = edges.shape[1]
    halo = halo.astype(F32)
    edges[0] = halo
    if side == 0:
        edges[1, pl.ds(0, edge - 4), :] = halo[4:]
    else:
        edges[1, pl.ds(4, edge - 4), :] = halo[: edge - 4]


def inner_kernel(
    core_ref, fields_ref, near_ref, kernel_ref, up_hbm, down_hbm, out_ref, upt_ref, downt_ref,
    s0, s4, kb, edges, up_ref, down_ref, sems,
):
    rows, cols, channels = fields_ref.shape
    taps = kernel_ref.shape[0]
    copies = [
        pltpu.make_async_copy(up_hbm, up_ref, sems.at[0]),
        pltpu.make_async_copy(down_hbm, down_ref, sems.at[1]),
    ]
    for copy in copies:
        copy.start()
    spread_taps(kb, kernel_ref, False)
    s4[...] = jnp.zeros_like(s4)
    edges[...] = jnp.zeros_like(edges)

    def one_row(side, r, carry):
        middle = fields_ref[r].astype(F32)
        s0[...] = middle
        s4[pl.ds(4, cols), :] = middle
        stage_edges(edges, near_ref[r], side)
        for lane in lane_groups(channels):
            lanes = pl.ds(lane * 128, 128)
            weights = [kb[t, :, lanes] for t in range(taps)]
            acc = [None] * (cols // 8)
            for i in range(cols // 8 + 1):
                for half, ref in ((0, s0), (1, s4)):
                    if half == 0 and i == cols // 8:
                        continue
                    x = ref[pl.ds(8 * i, 8), lanes]
                    for j in range(cols // 8):
                        t = 2 * (i - j) - half + taps // 2
                        if 0 <= t < taps:
                            add_to(acc, j, weights[t] * x)
            for j, value in halo_terms(edges, kb, lane, cols, taps, side).items():
                add_to(acc, j, value)
            for j, value in enumerate(acc):
                out_ref[r, pl.ds(8 * j, 8), lanes] = value
        return carry

    for side, here in ((1, core_ref[0] == 0), (0, core_ref[0] != 0)):

        @pl.when(here)
        def _(side=side):
            lax.fori_loop(0, rows, functools.partial(one_row, side), 0)

    for copy in copies:
        copy.wait()


def inner(core, fields, near, kernel, up, down):
    rows, cols, channels = fields.shape
    taps, edge = kernel.shape[0], near.shape[1]
    return pl.pallas_call(
        inner_kernel,
        in_specs=[pl.BlockSpec(memory_space=pltpu.SMEM)]
        + [resident()] * 3
        + [pl.BlockSpec(memory_space=pltpu.HBM)] * 2,
        out_specs=[resident()] * 3,
        out_shape=[resident_shape(rows, cols, channels), pltpu.VMEM(down.shape, BF16), pltpu.VMEM(up.shape, BF16)],
        scratch_shapes=[
            pltpu.VMEM((cols, channels), F32),
            pltpu.VMEM((cols + 8, channels), F32),
            pltpu.VMEM((taps, 8, channels), F32),
            pltpu.VMEM((2, edge, channels), F32),
            pltpu.VMEM(up.shape, BF16),
            pltpu.VMEM(down.shape, BF16),
            pltpu.SemaphoreType.DMA((2,)),
        ],
        compiler_params=pltpu.CompilerParams(vmem_limit_bytes=8 * 2**20),
        cost_estimate=pl.CostEstimate(
            flops=260 * taps * rows * cols * channels, transcendentals=0,
            bytes_accessed=rows * cols * channels * 6,
        ),
        name="inner",
    )(core, fields, near, kernel, up, down)


def forward_kernel(
    reach, first, last, start, core_ref, inner_ref, far_ref, fields_ref, cot_ref, kernel_ref,
    up_ref, upt_ref, down_ref, downt_ref, *refs,
):
    given, refs = ((), refs) if first else (refs[2:4], refs[4:])
    (out_ref, grad_ref, gup_ref, gdt_ref), refs = refs[:4], refs[4:]
    if reach:
        (near_out_ref, far_out_ref), refs = refs[:2], refs[2:]
        edges, kb, conv_s = refs[:3]
        refs = refs[3:]
    normed_s, act_s, hg_s = refs[:3]
    gup_s, gdt_s = refs[3:] if last else (gup_ref, gdt_ref)
    step = pl.program_id(0)
    _, cols, channels = inner_ref.shape
    edge, taps = far_ref.shape[1], kernel_ref.shape[0]
    rows = far_ref.shape[0] if reach else NEAR_BLOCK
    base_row = start + step * rows
    here = pl.ds(base_row, rows)
    even = core_ref[0] == 0
    hid = up_ref.shape[1]
    width = 256
    count = edge if reach else cols - edge
    cells = rows * count
    if reach:
        place = jnp.where(even, 0, cols - edge)
    else:
        place = jnp.where(even, edge, 0)
    span = pl.ds(pl.multiple_of(place, 16), count)

    @pl.when(step == 0)
    def _():
        if first:
            gup_s[...] = jnp.zeros_like(gup_s)
            gdt_s[...] = jnp.zeros_like(gdt_s)
        if last:
            gup_s[...] = given[0][...]
            gdt_s[...] = given[1][...]
        if reach:
            spread_taps(kb, kernel_ref, False)
            edges[...] = jnp.zeros_like(edges)

    if reach:

        def one_row(side, r, carry):
            stage_edges(edges, far_ref[r], side)
            for lane in lane_groups(channels):
                lanes = pl.ds(lane * 128, 128)
                terms = halo_terms(edges, kb, lane, cols, taps, side)
                skip = (cols - edge) // 8 if side else 0
                for j in range(count // 8):
                    base = inner_ref[base_row + r, pl.ds(8 * (j + skip), 8), lanes]
                    conv_s[r, pl.ds(8 * j, 8), lanes] = base + terms[j + skip] if j + skip in terms else base
            return carry

        for side, mine in ((0, even), (1, jnp.logical_not(even))):

            @pl.when(mine)
            def _(side=side):
                lax.fori_loop(0, rows, functools.partial(one_row, side), 0)

        conv = conv_s[...].reshape(cells, channels)
    else:
        conv = inner_ref[here, span, :].reshape(cells, channels)
    center = jnp.mean(conv, axis=-1, keepdims=True)
    deviation = conv - center
    spread = jnp.mean(deviation * deviation, axis=-1, keepdims=True)
    inv_scale = lax.rsqrt(spread + 1e-06)
    normed = deviation * inv_scale
    normed_s[...] = normed
    low = normed.astype(BF16)
    cot = cot_ref[here, span, :].reshape(cells, channels)
    over_cells, over_last = (((0,), (0,)), ((), ())), (((1,), (1,)), ((), ()))
    for j in range(hid // width):
        part = pl.ds(j * width, width)
        h = jnp.dot(low, up_ref[:, part], preferred_element_type=F32)
        u = lax.dot_general(cot, down_ref[part, :], over_last, preferred_element_type=F32)
        inner = h * (GELU_A + GELU_B * (h * h))
        t = jnp.tanh(inner)
        rise = 1.0 + t
        act_s[:, part] = (0.5 * h * rise).astype(BF16)
        slope = rise * (0.5 + (1.0 - t) * (1.5 * inner - GELU_A * h))
        hg_s[:, part] = (u * slope).astype(BF16)
    out = jnp.dot(act_s[...], down_ref[...], preferred_element_type=F32)
    out = out + fields_ref[here, span, :].reshape(cells, channels).astype(F32)
    normed_grad = lax.dot_general(hg_s[...], up_ref[...], over_last, preferred_element_type=F32)
    for j in range(hid // width):
        part = pl.ds(j * width, width)
        gup_s[j] += lax.dot_general(low, hg_s[:, part], over_cells, preferred_element_type=F32)
        gdt_s[:, part] += lax.dot_general(cot, act_s[:, part], over_cells, preferred_element_type=F32)
    out_ref[here, span, :] = out.astype(BF16).reshape(rows, count, channels)
    normed = normed_s[...]
    mean_grad = jnp.mean(normed_grad, axis=-1, keepdims=True)
    mean_cross = jnp.mean(normed_grad * normed, axis=-1, keepdims=True)
    grad = inv_scale * (normed_grad - mean_grad - normed * mean_cross)
    grad = grad.reshape(rows, count, channels)
    grad_ref[here, span, :] = grad
    if reach:
        far_out_ref[...] = grad.astype(BF16)
        near_place = jnp.where(even, cols - edge, 0)
        near_out_ref[...] = grad_ref[here, pl.ds(pl.multiple_of(near_place, 16), edge), :].astype(BF16)

    if last:
        mine_ref, theirs_ref = gup_ref, gdt_ref
        ending = step == pl.num_programs(0) - 1

        @pl.when(ending & even)
        def _():
            for j in range(hid // width):
                part = pl.ds(j * width, width)
                mine_ref[part, :] = gup_s[j]
                theirs_ref[part, :] = gdt_s[:, part].T.astype(BF16)

        @pl.when(ending & jnp.logical_not(even))
        def _():
            for j in range(hid // width):
                part = pl.ds(j * width, width)
                theirs_ref[part, :] = gup_s[j].astype(BF16)
                mine_ref[part, :] = gdt_s[:, part].T


def forward(core, conv_inner, far, fields, cot, kernel, up, up_t, down, down_t, carried, reach, begin, end):
    rows, cols, channels = cot.shape
    edge = far.shape[1]
    taps, hid = kernel.shape[0], up.shape[1]
    count = edge if reach else cols - edge
    cells = (end - begin) * count
    last = reach and end == rows
    block = end - begin if reach else NEAR_BLOCK
    own = row_spec(block, edge, channels)
    sums = [(hid // 256, channels, 256), (channels, hid)]
    ends = [((hid, channels), F32), ((hid, channels), BF16)] if last else [(s, F32) for s in sums]
    edges_out = [jax.ShapeDtypeStruct((end - begin, edge, channels), BF16)] * (2 if reach else 0)
    block_cells = block * count
    return pl.pallas_call(
        functools.partial(forward_kernel, reach, not carried, last, begin),
        grid=((end - begin) // block,),
        in_specs=[pl.BlockSpec(memory_space=pltpu.SMEM), resident(), own if reach else resident()]
        + [resident()] * (7 + len(carried)),
        out_specs=[resident()] * 4 + [own] * len(edges_out),
        out_shape=[pltpu.VMEM((rows, cols, channels), BF16), resident_shape(rows, cols, channels)]
        + [pltpu.VMEM(s, d) for s, d in ends]
        + edges_out,
        input_output_aliases={} if not carried else {10: 0, 11: 1} if last else {10: 0, 11: 1, 12: 2, 13: 3},
        scratch_shapes=(
            [
                pltpu.VMEM((2, edge, channels), F32),
                pltpu.VMEM((taps, 8, channels), F32),
                pltpu.VMEM((block, count, channels), F32),
            ]
            if reach
            else []
        )
        + [
            pltpu.VMEM((block_cells, channels), F32),
            pltpu.VMEM((block_cells, hid), BF16),
            pltpu.VMEM((block_cells, hid), BF16),
        ]
        + ([pltpu.VMEM(s, F32) for s in sums] if last else []),
        compiler_params=params(28),
        cost_estimate=pl.CostEstimate(
            flops=28 * cells * channels * hid, transcendentals=cells * hid,
            bytes_accessed=cells * channels * 12,
        ),
        name="forward",
    )(core, conv_inner, far, fields, cot, kernel, up, up_t, down, down_t, *carried)


def kernel_grad_kernel(start, core_ref, fields_ref, near_ref, far_ref, grad_ref, given_ref, out_ref, s0, s4, sums):
    _, cols, channels = fields_ref.shape
    rows, edge, _ = far_ref.shape
    even = core_ref[0] == 0
    taps = out_ref.shape[0] - 1
    blocks = cols // 8

    sums[...] = jnp.zeros_like(sums)

    def one_row(r, carry):
        left, right = halo_row(even, near_ref[start + r], far_ref[r])
        stage_row(s0, s4, left, fields_ref[start + r], right)
        for lane in lane_groups(channels):
            lanes = pl.ds(lane * 128, 128)
            grads = [grad_ref[start + r, pl.ds(8 * j, 8), lanes] for j in range(blocks)]
            acc = [None] * taps
            for i, half, uses in tap_uses(blocks, taps, edge):
                x = (s4 if half else s0)[pl.ds(8 * i, 8), lanes]
                for j, t in uses:
                    add_to(acc, t, grads[j] * x)
            for t in range(taps):
                sums[t, :, lanes] += acc[t]
        return carry

    lax.fori_loop(0, rows, one_row, 0)

    for t in range(taps):
        here = jnp.sum(sums[t], axis=0, keepdims=True)
        out_ref[pl.ds(t, 1), :] = given_ref[pl.ds(t, 1), :] + here
    out_ref[pl.ds(taps, 1), :] = jnp.zeros((1, channels), F32)


def staging(cols, edge, channels):
    return [
        pltpu.VMEM((cols + 2 * edge, channels), F32),
        pltpu.VMEM((cols + 2 * edge - 8, channels), F32),
    ]


def kernel_grad(core, fields, near, far, grad, given, start):
    _, cols, channels = fields.shape
    count, edge, _ = far.shape
    taps = given.shape[0] - 1
    return pl.pallas_call(
        functools.partial(kernel_grad_kernel, start),
        in_specs=[pl.BlockSpec(memory_space=pltpu.SMEM)] + [resident()] * 5,
        out_specs=resident(),
        out_shape=resident_shape(taps + 1, channels),
        scratch_shapes=staging(cols, edge, channels) + [pltpu.VMEM((taps, 8, channels), F32)],
        compiler_params=pltpu.CompilerParams(vmem_limit_bytes=8 * 2**20),
        cost_estimate=pl.CostEstimate(
            flops=60 * taps * count * cols * channels, transcendentals=0,
            bytes_accessed=count * cols * channels * 8,
        ),
        name="kernel_grad",
    )(core, fields, near, far, grad, given)


def backward_kernel(start, core_ref, grad_ref, near_ref, far_ref, cot_ref, kernel_ref, *refs):
    out_ref, s0, s4, kb = refs[-4:]
    _, cols, channels = grad_ref.shape
    rows, edge, _ = far_ref.shape
    even = core_ref[0] == 0
    base = start + pl.program_id(0) * rows
    taps = kernel_ref.shape[0]

    @pl.when(pl.program_id(0) == 0)
    def _():
        spread_taps(kb, kernel_ref, True)

    def one_row(r, carry):
        left, right = halo_row(even, near_ref[base + r], far_ref[r])
        stage_row(s0, s4, left, grad_ref[base + r], right)
        for lane in lane_groups(channels):
            acc = conv_lane(s0, s4, kb, lane, cols, taps, edge)
            lanes = pl.ds(lane * 128, 128)
            back = jnp.concatenate(acc, axis=0) + cot_ref[r, :, lanes].astype(F32)
            out_ref[r, :, lanes] = back.astype(BF16)
        return carry

    lax.fori_loop(0, rows, one_row, 0)


def backward(core, grad, near, far, cot, kernel, carried, start):
    rows, cols, channels = grad.shape
    count, edge, _ = far.shape
    taps = kernel.shape[0]
    own = functools.partial(row_spec, BLOCK)
    at = pl.BlockSpec((BLOCK, cols, channels), lambda i: (i + start // BLOCK, 0, 0))
    return pl.pallas_call(
        functools.partial(backward_kernel, start),
        grid=(count // BLOCK,),
        in_specs=[
            pl.BlockSpec(memory_space=pltpu.SMEM), resident(), resident(), own(edge, channels), at, resident(),
        ]
        + [pl.BlockSpec(memory_space=pl.ANY)] * len(carried),
        out_specs=at,
        out_shape=jax.ShapeDtypeStruct((rows, cols, channels), BF16),
        input_output_aliases={6: 0} if carried else {},
        scratch_shapes=staging(cols, edge, channels) + [pltpu.VMEM((taps, 8, channels), F32)],
        compiler_params=params(8),
        cost_estimate=pl.CostEstimate(
            flops=60 * taps * count * cols * channels, transcendentals=0,
            bytes_accessed=count * cols * channels * 10,
        ),
        name="backward",
    )(core, grad, near, far, cot, kernel, *carried)


def finish_kernel(factor, core_ref, own_ref, got_ref, tail_ref, kgrad_ref, up_ref, down_ref, taps_ref):
    even = core_ref[0] == 0
    width = own_ref.shape[1]
    for j in range(own_ref.shape[0] // width):
        part = pl.ds(j * width, width)
        own, got = own_ref[part, :].astype(F32) * factor, got_ref[part, :].astype(F32) * factor
        up_ref[:, part] = jnp.where(even, own, got)
        down_ref[part, :] = jnp.where(even, got, own)
    taps = taps_ref.shape[0]
    taps_ref[...] = (kgrad_ref[pl.ds(0, taps), :] + tail_ref[pl.ds(0, taps), :].astype(F32)) * factor


def finish(core, own, got, kgrad, taps, factor):
    hid, channels = own.shape[0] - kgrad.shape[0], own.shape[1]
    rows = hid // 2
    part = pl.BlockSpec((rows, channels), lambda j: (j, 0))
    return pl.pallas_call(
        functools.partial(finish_kernel, factor),
        grid=(hid // rows,),
        in_specs=[
            pl.BlockSpec(memory_space=pltpu.SMEM), part, part,
            pl.BlockSpec(kgrad.shape, lambda j: (hid // kgrad.shape[0], 0)), whole_spec(*kgrad.shape),
        ],
        out_specs=[
            pl.BlockSpec((channels, rows), lambda j: (0, j)), part, whole_spec(taps, channels),
        ],
        out_shape=[
            jax.ShapeDtypeStruct((channels, hid), F32),
            jax.ShapeDtypeStruct((hid, channels), F32),
            jax.ShapeDtypeStruct((taps, channels), F32),
        ],
        compiler_params=params(8),
        name="finish",
    )(core, own, got, got, kgrad)


def after(values, *others):
    held, _ = lax.optimization_barrier((values, others))
    return held


def chunk_starts(rows):
    first = rows // 2 // BLOCK * BLOCK
    return [0, first, rows]


def with_places(fields):
    found = groups()
    core = found[0][0][0]
    fields, places, index, even = lax.optimization_barrier(
        (fields, [places for places, _ in found], core.astype(jnp.int32).reshape(1), core == 0)
    )
    return fields, [(p, masks) for p, (_, masks) in zip(places, found)], index, even


def per_device(fields, cotangent, kernel, up_weight, down_weight):
    rows, cols, channels = fields.shape
    taps, hid = kernel.shape[0], up_weight.shape[1]
    edge = -(-KERNEL_SPACING * (taps // 2) // 8) * 8
    fields, (core, plane, depth), index, even = with_places(fields)
    bounds = chunk_starts(rows)
    chunks = list(zip(bounds[:-1], bounds[1:]))
    to_left, to_right = fields[:, :edge], fields[:, cols - edge :]
    near_out, far_out = jnp.where(even, to_right, to_left), jnp.where(even, to_left, to_right)
    middle = chunks[0][1]
    near = on_chip(near_out)
    far = [off_chip(far_out[:middle])]
    near, _ = lax.optimization_barrier((near, far_out))
    conv_inner, up_t, down_t = inner(index, fields, near, kernel, up_weight, down_weight)
    far_out = after(far_out, conv_inner)
    far.append(off_chip(far_out[middle:]))

    def cells_of(carried, reach, halo, begin, end):
        return forward(
            index, conv_inner, halo, fields, cotangent, kernel, up_weight, up_t, down_weight, down_t,
            carried, reach, begin, end,
        )

    carried = cells_of((), False, near, 0, rows)
    grad_near, grad_far = [], []
    for (begin, end), arrived in zip(chunks, far):
        *carried, near_edge, far_edge = cells_of(carried, True, arrived, begin, end)
        grad_near.append(near_edge)
        if end < rows:
            grad_far.append(off_chip(far_edge))
    output, grad, mine, theirs = carried

    kgrad = jnp.zeros((taps + 1, channels), F32)

    def add_kernel_grad(total, which):
        return kernel_grad(index, fields, near, far[which], grad, total, chunks[which][0])

    def add_field_grad(so_far, which):
        return (
            backward(index, grad, grad_near, grad_far[which], cotangent, kernel, so_far, chunks[which][0]),
        )

    quarter = hid // 4
    got = [xor_permute(theirs[i : i + quarter], core[1][1]) for i in range(0, hid, quarter)]
    part = mine + jnp.concatenate(got, axis=0).astype(F32)
    sends, total = scatter_stage(part, plane)
    kgrad = after(kgrad, *sends)
    kgrad = add_kernel_grad(kgrad, 0)
    part, kgrad = scatter_finish(sends, total, plane, kgrad)
    part, far_edge = lax.optimization_barrier((part, far_edge))
    grad_far.append(off_chip(far_edge))
    grad_near = on_chip(jnp.concatenate(grad_near, axis=0))
    sends, total = scatter_stage(part, depth)
    sends = after(sends, grad_far[0])
    sends, kgrad = lax.optimization_barrier((sends, kgrad))
    kgrad = add_kernel_grad(kgrad, 1)
    part, kgrad = scatter_finish(sends, total, depth, kgrad)
    part = part.astype(BF16)
    packed = pack(part, kgrad)
    grad_far, _ = lax.optimization_barrier((grad_far, packed))
    field_grad = add_field_grad((), 0)
    part, kgrad, field_grad = gather_finish(packed, kgrad, depth, field_grad)
    packed = pack(part, kgrad)
    field_grad, grad_far[1] = lax.optimization_barrier((field_grad, after(grad_far[1], packed)))
    field_grad = add_field_grad(field_grad, 1)
    part, kgrad, field_grad = gather_finish(packed, kgrad, plane, field_grad)
    packed = pack(part, kgrad)
    got = on_chip(packed)
    factor = 1.0 / math.sqrt(rows * cols * lax.axis_size("lon") * lax.axis_size("lat"))
    up_grad, down_grad, tap_grad = finish(index, packed, got, kgrad, taps, factor)
    return (output, field_grad[0], tap_grad, up_grad, down_grad)


def solution(mesh):
    placed = (P("lat", "lon", None), P("lat", "lon", None), P(), P(), P())
    return jax.shard_map(
        per_device,
        mesh=mesh,
        in_specs=placed,
        out_specs=(P("lat", "lon", None), P("lat", "lon", None), P(), P(), P()),
        check_vma=False,
    )
```
